32 devices in a mesh: parts: 2 (over y), space: 4 (over z), section: 2 (over x), chan: 2 (over core).
Axes of the slice: x: 2, y: 2, z: 4, core: 2. Of those that a mesh axis runs over, the one named last changes fastest.
Arguments:
- section_inputs: bfloat16 [2, 6, 8, 16, 16, 128], P('section', 'parts', 'space'), parts along dimension 1, may hold values from -6 to 6
- cotangent: bfloat16 [6, 8, 16, 16, 128], P('parts', 'space'), parts along dimension 0, may hold values from -6 to 6
- phase_labels: int32 [6, 8, 16, 16], P('parts', 'space'), parts along dimension 0, may hold values from 0 to 2
- expand_weight: bfloat16 [2, 128, 256], P('section', None, 'chan'), may hold values from -0.5 to 0.5
- phase_code: float32 [2, 3, 256], P('section', None, 'chan'), may hold values from -6 to 6
- kernel: bfloat16 [2, 27, 32, 8, 8], P('section', None, 'chan'), may hold values from -0.4375 to 0.4375
- reduce_weight: bfloat16 [2, 256, 128], P('section', 'chan'), may hold values from -0.375 to 0.375
Outputs:
- input_grads: bfloat16 [2, 6, 8, 16, 16, 128], P('section', 'parts', 'space'), parts along dimension 1
- expand_grad: float32 [4, 128, 256], P(('parts', 'section'), None, 'chan'), parts along dimension 0
- kernel_grad: float32 [4, 27, 32, 8, 8], P(('parts', 'section'), None, 'chan'), parts along dimension 0
- reduce_grad: float32 [4, 256, 128], P(('parts', 'section'), 'chan'), parts along dimension 0
The draws below stay inside these ranges and needn't reach their ends.
There are 2 independent parts, one for each index of `parts`. The reference program is written for one: setup_inputs(seed, part) draws one part's arguments, and reference() takes and returns one part's arrays. A program takes and returns all parts, laid end to end along the dimension named above; an argument that names none is the same for every part. Nothing has to cross between parts.
All inputs are finite; a program needn't handle non-finite values.
Results may differ from the reference program's by a relative error of at most 0.015.
Values may be sent and summed in bfloat16 or wider, within the bound.
No kernel may reach another device: no remote copies, remote signals or barrier semaphores. Data moves between devices by JAX's collectives and lax.ppermute only.
A program may use at most 192 MiB of HBM per device.

```python
import math
import jax
import jax.numpy as jnp

CHANNELS = 128
BOTTLENECK = 256
GROUPS = 32
PER_GROUP = 8
PHASES = 3
MICROBATCH = 3
GRID_Y = 16
GRID_Z = 16
GRID_X = 8
SECTIONS = 2


def touch_ends(drawn, rng, smallest, top_value):
    extent = drawn.shape
    index_at = [jax.random.randint(jax.random.fold_in(rng, axis), (), 0, extent[axis]) for axis in range(len(extent))]
    drawn = drawn.at[tuple(index_at)].set(smallest)
    longest = extent.index(max(extent))
    index_at[longest] = (index_at[longest] + 1) % extent[longest]
    return drawn.at[tuple(index_at)].set(top_value)


def level_of(rng, extent, pieces, smallest, largest):
    loudness, own = 1.0, jax.random.fold_in(rng, 6)
    for dim, blocks in pieces:
        steps = jnp.exp(jax.random.uniform(jax.random.fold_in(own, dim), (blocks,), jnp.float32, smallest / len(pieces), largest / len(pieces)))
        loudness = loudness * jnp.repeat(steps, extent[dim] // blocks).reshape([-1 if axis == dim else 1 for axis in range(len(extent))])
    return loudness


def centred(own_key, shape, scale, most, split=(), held_as=jnp.bfloat16):
    gain = level_of(own_key, shape, split, -0.22, 0.18) if split else 1.0
    array = jax.random.normal(own_key, shape, jnp.float32) * scale * gain
    return jnp.minimum(jnp.maximum(array, -most), most).astype(held_as)


def setup_inputs(seed: int = 0, part: int = 0) -> dict:
    keys = jax.random.split(jax.random.key(seed), 8)
    part_keys = jax.random.split(jax.random.fold_in(keys[7], part), 8)
    return {
        "section_inputs": centred(part_keys[0], (SECTIONS, MICROBATCH, GRID_X, GRID_Y, GRID_Z, CHANNELS), 1.0, 6.0, ((0, 2), (2, 4))),
        "cotangent": centred(part_keys[1], (MICROBATCH, GRID_X, GRID_Y, GRID_Z, CHANNELS), 1.0, 6.0, ((1, 4),)),
        "phase_labels": touch_ends(jax.random.randint(part_keys[2], (MICROBATCH, GRID_X, GRID_Y, GRID_Z), 0, PHASES), jax.random.fold_in(part_keys[2], 1), 0, PHASES - 1).astype(jnp.int32),
        "expand_weight": centred(keys[3], (SECTIONS, CHANNELS, BOTTLENECK), CHANNELS ** -0.5, 0.5, ((0, 2), (2, 2))),
        "phase_code": centred(keys[4], (SECTIONS, PHASES, BOTTLENECK), 1.0, 6.0, ((0, 2), (2, 2)), jnp.float32),
        "kernel": centred(keys[5], (SECTIONS, 27, GROUPS, PER_GROUP, PER_GROUP), (27 * PER_GROUP) ** -0.5, 0.4375, ((0, 2), (2, 2))),
        "reduce_weight": centred(keys[6], (SECTIONS, BOTTLENECK, CHANNELS), BOTTLENECK ** -0.5, 0.375, ((0, 2), (1, 2))),
    }


tap_offsets = [(first, second, third) for first in (-1, 0, 1) for second in (-1, 0, 1) for third in (-1, 0, 1)]

def silu_slope(value):
    sigma = jax.nn.sigmoid(value)
    return sigma * (1.0 + value * (1.0 - sigma))

def reference(section_inputs, cotangent, phase_labels, expand_weight, phase_code, kernel, reduce_weight):
    cell_count = GRID_X * GRID_Y * GRID_Z
    norm_scale = 1.0 / math.sqrt(MICROBATCH * cell_count)
    five_shape = (GRID_X, GRID_Y, GRID_Z, GROUPS, PER_GROUP)
    upstream_list = [cotangent[batch_id] for batch_id in range(MICROBATCH)]
    grads_in = [None] * SECTIONS
    expand_list = [None] * SECTIONS
    kernel_list = [None] * SECTIONS
    reduce_list = [None] * SECTIONS
    for section_id in range(SECTIONS - 1, -1, -1):
        kernel_here = kernel[section_id].astype(jnp.float32)
        expand_acc = jnp.zeros((CHANNELS, BOTTLENECK), jnp.float32)
        kernel_acc = jnp.zeros((27, GROUPS, PER_GROUP, PER_GROUP), jnp.float32)
        reduce_acc = jnp.zeros((BOTTLENECK, CHANNELS), jnp.float32)
        outputs_here = []
        for batch_id in range(MICROBATCH):
            flat_in = section_inputs[section_id, batch_id].reshape(cell_count, CHANNELS)
            code_rows = phase_code[section_id][phase_labels[batch_id].reshape(-1).astype(jnp.int32)]
            pre_act = jnp.dot(flat_in, expand_weight[section_id], preferred_element_type=jnp.float32) + code_rows
            hidden = jax.nn.silu(pre_act).astype(jnp.bfloat16).reshape(five_shape)
            conv_out = jnp.zeros(five_shape, jnp.float32)
            for tap_id, offset in enumerate(tap_offsets):
                moved = jnp.roll(hidden, (-offset[0], -offset[1], -offset[2]), axis=(0, 1, 2)).astype(jnp.float32)
                conv_out = conv_out + jnp.einsum('xyzgi,gio->xyzgo', moved, kernel_here[tap_id])
            conv_flat = conv_out.reshape(cell_count, BOTTLENECK)
            mixed_out = jax.nn.silu(conv_flat).astype(jnp.bfloat16)
            flat_up = upstream_list[batch_id].reshape(cell_count, CHANNELS)
            grad_mixed = jnp.dot(flat_up, reduce_weight[section_id].T, preferred_element_type=jnp.float32)
            reduce_acc = reduce_acc + jnp.dot(mixed_out.T, flat_up, preferred_element_type=jnp.float32)
            grad_conv = (grad_mixed * silu_slope(conv_flat)).astype(jnp.bfloat16)
            grad_five = grad_conv.reshape(five_shape).astype(jnp.float32)
            grad_hidden = jnp.zeros(five_shape, jnp.float32)
            for tap_id, offset in enumerate(tap_offsets):
                moved = jnp.roll(hidden, (-offset[0], -offset[1], -offset[2]), axis=(0, 1, 2)).astype(jnp.float32)
                kernel_acc = kernel_acc.at[tap_id].add(jnp.einsum('xyzgi,xyzgo->gio', moved, grad_five))
                backward = jnp.roll(grad_five, (offset[0], offset[1], offset[2]), axis=(0, 1, 2))
                grad_hidden = grad_hidden + jnp.einsum('xyzgo,gio->xyzgi', backward, kernel_here[tap_id])
            grad_pre = (grad_hidden.reshape(cell_count, BOTTLENECK) * silu_slope(pre_act)).astype(jnp.bfloat16)
            expand_acc = expand_acc + jnp.dot(flat_in.T, grad_pre, preferred_element_type=jnp.float32)
            branch = jnp.dot(grad_pre, expand_weight[section_id].T, preferred_element_type=jnp.float32)
            result = (flat_up.astype(jnp.float32) + branch).astype(jnp.bfloat16)
            outputs_here.append(result.reshape(GRID_X, GRID_Y, GRID_Z, CHANNELS))
        upstream_list = outputs_here
        grads_in[section_id] = jnp.stack(outputs_here)
        expand_list[section_id] = expand_acc * norm_scale
        kernel_list[section_id] = kernel_acc * norm_scale
        reduce_list[section_id] = reduce_acc * norm_scale
    return (jnp.stack(grads_in), jnp.stack(expand_list), jnp.stack(kernel_list), jnp.stack(reduce_list))
```

```python
import functools
import math

import jax
import jax.numpy as jnp
from jax import lax
from jax.experimental import pallas as pl
from jax.experimental.pallas import tpu as pltpu
from jax.sharding import PartitionSpec as P

BF = jnp.bfloat16
F32 = jnp.float32
LANES = 128


def gate(v):
    return 0.5 + 0.5 * jnp.tanh(0.5 * v)


def slope(v, q):
    return q * (1.0 + v * (1.0 - q))


def nt_dot(a, b):
    return lax.dot_general(a, b, (((1,), (1,)), ((), ())), preferred_element_type=F32)


def store_shifts(ref, plane, value, wide, deep):
    cells = wide * deep
    cube = value.reshape(wide, deep, LANES)
    for j, turn in enumerate((1, 0, deep - 1)):
        moved = cube if turn == 0 else pltpu.roll(cube, turn, axis=1)
        flat = moved.reshape(cells, LANES).astype(BF)
        lanes = slice(j * LANES, (j + 1) * LANES)
        ref[plane, deep : deep + cells, lanes] = flat
        ref[plane, 0:deep, lanes] = flat[cells - deep :]
        ref[plane, deep + cells : cells + 2 * deep, lanes] = flat[:deep]


def views(ref, plane, cells, deep):
    return [
        ref[plane + dx, (1 + dy) * deep : (1 + dy) * deep + cells, :]
        for dx in (-1, 0, 1)
        for dy in (-1, 0, 1)
    ]


def conv_plane(ref, plane, weights, cells, deep):
    rows = jnp.concatenate(views(ref, plane, cells, deep), axis=1)
    return jnp.dot(rows, weights[...], preferred_element_type=F32)


def pack_kernel(micro, cells, wide, x_ref, ct_ref, lab_ref, *outs):
    c = lax.axis_index("chan")
    for m in range(micro):
        a_ref, b_ref = outs[2 * m], outs[2 * m + 1]
        x = x_ref[m, c]
        lab = lab_ref[m, c]
        a_ref[0:cells] = x
        a_ref[cells : cells + wide] = lab
        a_ref[cells + wide : 2 * cells + wide] = ct_ref[m, c]
        b_ref[0:cells] = x
        b_ref[cells : cells + wide] = lab


def weights_kernel(taps, width, kf_ref, kb_ref, f_ref, b_ref):
    groups = LANES // width
    g = lax.broadcasted_iota(jnp.int32, (groups, width, LANES), 0)
    lane = lax.broadcasted_iota(jnp.int32, (groups, width, LANES), 2)
    keep = g == lane // width
    for src, dst in ((kf_ref, f_ref), (kb_ref, b_ref)):
        for t in range(taps):
            one = src[t * width : (t + 1) * width, :]
            full = jnp.where(keep, jnp.broadcast_to(one[None], keep.shape), 0.0)
            dst[t * LANES : (t + 1) * LANES, :] = full.reshape(LANES, LANES).astype(BF)


def forward_kernel(
    wide,
    deep,
    x_ref,
    lab_ref,
    a_ref,
    b_ref,
    a2_ref,
    b2_ref,
    ct_ref,
    w_ref,
    code_ref,
    rw_ref,
    kf_ref,
    kb_ref,
    hid_ref,
    spre_ref,
    sconv_ref,
    mixed_ref,
    base_ref,
    other_ref,
    hs_ref,
    gs_ref,
    br_ref,
):
    c = lax.axis_index("chan")
    cells = wide * deep
    low, high = 1 - c, c
    codes = [jnp.broadcast_to(code_ref[i : i + 1, :], (deep, LANES)) for i in range(3)]

    def hidden_of(x, lab, plane, own):
        pre = jnp.dot(x, w_ref[...], preferred_element_type=F32)
        lab = lab.astype(F32)
        adds = []
        for y in range(wide):
            tag = jnp.broadcast_to(lab[:, y : y + 1], (deep, LANES))
            adds.append(jnp.where(tag < 0.5, codes[0], jnp.where(tag < 1.5, codes[1], codes[2])))
        pre = pre + jnp.concatenate(adds, axis=0)
        q = gate(pre)
        h = pre * q
        if own is not None:
            hid_ref[own] = h.astype(BF)
            spre_ref[own] = slope(pre, q)
        store_shifts(hs_ref, plane, h, wide, deep)

    hidden_of(x_ref[0, 0], lab_ref[0, 0], 2, 0)
    hidden_of(x_ref[0, 1], lab_ref[0, 1], 3, 1)
    for ref, plane in (
        (a_ref, 4 - 3 * c),
        (b_ref, 5 * c),
        (a2_ref, 1 + 3 * c),
        (b2_ref, 5 - 5 * c),
    ):
        hidden_of(ref[0:cells], ref[cells : cells + wide], plane, None)

    for p in range(4):
        conv = conv_plane(hs_ref, p + 1, kf_ref, cells, deep)
        q = gate(conv)
        sconv_ref[p] = slope(conv, q)
        if p in (1, 2):
            mixed_ref[p - 1] = (conv * q).astype(BF)

    ups = (
        (ct_ref[0, 0], 1),
        (ct_ref[0, 1], 2),
        (a_ref[cells + wide : 2 * cells + wide], 3 - 3 * c),
        (a2_ref[cells + wide : 2 * cells + wide], 3 * c),
    )
    for up, plane in ups:
        grad = nt_dot(up, rw_ref[...]) * sconv_ref[plane]
        store_shifts(gs_ref, plane, grad.astype(BF).astype(F32), wide, deep)
    for p in (0, 1):
        grad_hidden = conv_plane(gs_ref, p + 1, kb_ref, cells, deep)
        grad_pre = (grad_hidden * spre_ref[p]).astype(BF)
        br_ref[p] = nt_dot(grad_pre, w_ref[...])
    base_ref[...] = ct_ref[0, c].astype(F32) + br_ref[c]
    other_ref[...] = br_ref[1 - c].astype(BF)


def backward_kernel(
    full,
    wide,
    deep,
    taps,
    width,
    x_ref,
    ct_ref,
    cta_ref,
    cta2_ref,
    st_ref,
    st2_ref,
    dg_ref,
    dg2_ref,
    hid_ref,
    spre_ref,
    sconv_ref,
    mixed_ref,
    w_ref,
    rw_ref,
    kb_ref,
    *rest,
):
    c = lax.axis_index("chan")
    cells = wide * deep
    if full:
        exp_in, red_in, kg_in, part_ref, up_ref, exp_ref, red_ref, kg_ref, gs_ref = rest
    else:
        base_ref, other_ref, gs_ref, up_ref, br_ref = rest
    last = lax.axis_index("section") == lax.axis_size("section") - 1

    @pl.when(last)
    def _():
        up_ref[0] = ct_ref[0, 0]
        up_ref[1] = ct_ref[0, 1]

    @pl.when(jnp.logical_not(last))
    def _():
        up_ref[c] = st_ref[...]
        up_ref[1 - c] = st2_ref[...]

    tail = slice(cells + wide, 2 * cells + wide)
    halo = jnp.where(last, cta_ref[tail], dg_ref[...])
    halo2 = jnp.where(last, cta2_ref[tail], dg2_ref[...])
    ups = ((up_ref[0], 1), (up_ref[1], 2), (halo, 3 - 3 * c), (halo2, 3 * c))
    for up, plane in ups:
        grad = nt_dot(up, rw_ref[...]) * sconv_ref[plane]
        store_shifts(gs_ref, plane, grad.astype(BF).astype(F32), wide, deep)
    if full:
        ups2 = up_ref[...].reshape(2 * cells, LANES)
        red = lax.dot_general(
            mixed_ref[...].reshape(2 * cells, LANES),
            ups2,
            (((0,), (0,)), ((), ())),
            preferred_element_type=F32,
        )
        red_ref[...] = red_in[...] + red
        groups = LANES // width
        g = lax.broadcasted_iota(jnp.int32, (groups, width, LANES), 0)
        lane = lax.broadcasted_iota(jnp.int32, (groups, width, LANES), 2)
        keep = g == lane // width
        turned = [hid_ref[p].T for p in (0, 1)]
        left = jnp.concatenate(turned, axis=1)
        for dx in (-1, 0, 1):
            for dy in (-1, 0, 1):
                rows = slice((1 + dy) * deep, (1 + dy) * deep + cells)
                right = jnp.concatenate([gs_ref[1 + dx, rows, :], gs_ref[2 + dx, rows, :]], axis=0)
                dense = jnp.dot(left, right, preferred_element_type=F32)
                for j in range(3):
                    tap = 9 * (dx + 1) + 3 * (dy + 1) + j
                    block = dense[:, j * LANES : (j + 1) * LANES].reshape(groups, width, LANES)
                    thin = jnp.sum(jnp.where(keep, block, 0.0), axis=0)
                    at = slice((taps - 1 - tap) * width, (taps - tap) * width)
                    kg_ref[at] = kg_in[at] + thin
    grads = []
    for p in (0, 1):
        grad_hidden = conv_plane(gs_ref, p + 1, kb_ref, cells, deep)
        grad_pre = (grad_hidden * spre_ref[p]).astype(BF)
        branch = nt_dot(grad_pre, w_ref[...])
        if full:
            part_ref[p] = branch.astype(BF)
            grads.append(grad_pre)
        else:
            br_ref[p] = branch
    if full:
        exp_ref[...] = exp_in[...] + lax.dot_general(
            x_ref[0].reshape(2 * cells, LANES),
            jnp.concatenate(grads, axis=0),
            (((0,), (0,)), ((), ())),
            preferred_element_type=F32,
        )
    else:
        base_ref[...] = up_ref[c].astype(F32) + br_ref[c]
        other_ref[...] = br_ref[1 - c].astype(BF)


def finish_kernel(micro, count, scale, *refs):
    ins, outs = refs[: 3 * micro + count], refs[3 * micro + count : -1]
    buf = refs[-1]
    for m in range(micro):
        up, mine, other = ins[3 * m : 3 * m + 3]
        both = mine[...].astype(F32) + other[...].astype(F32)
        outs[0][m] = (up[...].astype(F32) + both).astype(BF)
    rank = lax.axis_index("space")
    for d in range(count):
        buf[lax.rem(rank + count - d, count)] = ins[3 * micro + d][...]
    total = buf[0].astype(F32)
    for d in range(1, count):
        total = total + buf[d].astype(F32)
    total = total * scale
    outs[1][...] = total[0:LANES]
    outs[2][...] = total[LANES : 2 * LANES]
    outs[3][...] = total[2 * LANES :]


def sds(shape, dtype):
    return jax.ShapeDtypeStruct(shape, dtype)


def params():
    return pltpu.CompilerParams(vmem_limit_bytes=40 * 2**20)


def cost(flops, nbytes):
    return pl.CostEstimate(flops=flops, bytes_accessed=nbytes, transcendentals=0)


def whole(shape):
    return pl.BlockSpec(shape, lambda i: (0,) * len(shape))


def picked(shape, m):
    return pl.BlockSpec((1,) + shape, lambda i: (m,) + (0,) * len(shape))


def on_device(
    section_inputs, cotangent, phase_labels, expand_weight, phase_code, kernel, reduce_weight
):
    _, micro, depth, wide, deep, trunk = section_inputs.shape
    cells = wide * deep
    taps, groups, width = kernel.shape[1], kernel.shape[2], kernel.shape[3]
    assert depth == 2 and lax.axis_size("chan") == 2
    assert trunk == LANES and groups * width == LANES
    spaces, sections = lax.axis_size("space"), lax.axis_size("section")
    scale = 1.0 / math.sqrt(micro * depth * spaces * cells)

    x = section_inputs[0].reshape(micro, depth, cells, trunk)
    ct = cotangent.reshape(micro, depth, cells, trunk)
    lab = jnp.swapaxes(phase_labels, 2, 3).astype(BF)
    lab = jnp.pad(lab, ((0, 0), (0, 0), (0, 0), (0, LANES - wide)))
    w, rw = expand_weight[0], reduce_weight[0]
    code = jnp.pad(phase_code[0], ((0, 8 - phase_code.shape[1]), (0, 0)))
    kern = kernel[0].astype(F32)
    kf = kern.transpose(0, 2, 1, 3).reshape(taps * width, LANES)
    kb = kern[::-1].transpose(0, 3, 1, 2).reshape(taps * width, LANES)

    away = [(k, c, (k + 2 * c - 1) % spaces) for k in range(spaces) for c in (0, 1)]
    back = [(k, c, (k - 2 * c + 1) % spaces) for k in range(spaces) for c in (0, 1)]
    route_a = [(2 * k + c, 2 * t + c) for k, c, t in away]
    route_b = [(2 * k + c, 2 * t + c) for k, c, t in back]
    route_d = [
        ((k * sections + s) * 2 + c, (t * sections + s - 1) * 2 + c)
        for k, c, t in away
        for s in range(1, sections)
    ]
    route_s = [(s, s - 1) for s in range(1, sections)]

    def swap(v):
        return lax.ppermute(v, "chan", [(0, 1), (1, 0)])

    packed = pl.pallas_call(
        functools.partial(pack_kernel, micro, cells, wide),
        out_shape=[
            sds((n, LANES), BF)
            for _ in range(micro)
            for n in (2 * cells + wide, cells + wide)
        ],
        name="pack",
        cost_estimate=cost(0, 4 * 2**20),
        compiler_params=params(),
    )(x, ct, lab)
    halos = []
    for m in range(micro):
        a = lax.ppermute(packed[2 * m], ("space", "chan"), route_a)
        b = lax.ppermute(packed[2 * m + 1], ("space", "chan"), route_b)
        halos.append((a, b, swap(a), swap(b)))

    dense_f, dense_b = pl.pallas_call(
        functools.partial(weights_kernel, taps, width),
        out_shape=[sds((taps * LANES, LANES), BF)] * 2,
        name="weights",
        cost_estimate=cost(0, 2 * 2**20),
        compiler_params=params(),
    )(kf, kb)

    plane2, plane4 = (2, cells, LANES), (4, cells, LANES)
    pad_rows = cells + 2 * deep
    shape_a, shape_b = (2 * cells + wide, LANES), (cells + wide, LANES)
    square, tall = (LANES, LANES), (taps * LANES, LANES)
    saved, handed = [], []
    for m in range(micro):
        a, b, a2, b2 = halos[m]
        hid, spre, sconv, mixed, base, other = pl.pallas_call(
            functools.partial(forward_kernel, wide, deep),
            grid=(1,),
            in_specs=[
                picked(plane2, m),
                picked((2, deep, LANES), m),
                whole(shape_a),
                whole(shape_b),
                whole(shape_a),
                whole(shape_b),
                picked(plane2, m),
                whole(square),
                whole((8, LANES)),
                whole(square),
                whole(tall),
                whole(tall),
            ],
            out_specs=[
                whole(plane2),
                whole(plane2),
                whole(plane4),
                whole(plane2),
                whole((cells, LANES)),
                whole((cells, LANES)),
            ],
            out_shape=[
                sds(plane2, BF),
                sds(plane2, F32),
                sds(plane4, F32),
                sds(plane2, BF),
                sds((cells, LANES), F32),
                sds((cells, LANES), BF),
            ],
            scratch_shapes=[
                pltpu.VMEM((6, pad_rows, 3 * LANES), BF),
                pltpu.VMEM((4, pad_rows, 3 * LANES), BF),
                pltpu.VMEM(plane2, F32),
            ],
            name="forward",
            cost_estimate=cost(2 * 10**9, 5 * 2**20),
            compiler_params=params(),
        )(x, lab, a, b, a2, b2, ct, w, code, rw, dense_f, dense_b)
        saved.append((hid, spre, sconv, mixed))
        handed.append((base, other))

    def hand_over(base, other):
        out = (base + swap(other).astype(F32)).astype(BF)
        st = lax.ppermute(out, "section", route_s)
        dg = lax.ppermute(out, ("space", "section", "chan"), route_d)
        return st, swap(st), dg, swap(dg)

    def back_pass(full, m, ups, sums):
        hid, spre, sconv, mixed = saved[m]
        a, _, a2, _ = halos[m]
        st, st2, dg, dg2 = ups
        flat = (cells, LANES)
        in_specs = [
            picked(plane2, m),
            picked(plane2, m),
            whole(shape_a),
            whole(shape_a),
            whole(flat),
            whole(flat),
            whole(flat),
            whole(flat),
            whole(plane2),
            whole(plane2),
            whole(plane4),
            whole(plane2),
            whole(square),
            whole(square),
            whole(tall),
        ]
        scratch = [pltpu.VMEM((4, pad_rows, 3 * LANES), BF)]
        sum_shapes = [square, square, (taps * width, LANES)]
        if full:
            out_shape = [sds(plane2, BF), sds(plane2, BF)] + [sds(s, F32) for s in sum_shapes]
            in_specs = in_specs + [whole(s) for s in sum_shapes]
        else:
            out_shape = [sds(flat, F32), sds(flat, BF)]
            scratch = scratch + [pltpu.VMEM(plane2, BF), pltpu.VMEM(plane2, F32)]
        return pl.pallas_call(
            functools.partial(backward_kernel, full, wide, deep, taps, width),
            grid=(1,),
            in_specs=in_specs,
            out_specs=[whole(s.shape) for s in out_shape],
            out_shape=out_shape,
            scratch_shapes=scratch,
            name="backward" if full else "backward_light",
            cost_estimate=cost(2 * 10**9, 5 * 2**20),
            compiler_params=params(),
        )(x, ct, a, a2, st, st2, dg, dg2, hid, spre, sconv, mixed, w, rw, dense_b, *sums)

    rank = lax.axis_index("section")
    ups = [hand_over(*handed[m]) for m in range(micro)]
    for stage in range(1, sections - 1):
        fresh = [hand_over(*back_pass(False, m, ups[m], ())) for m in range(micro)]
        mine = rank == sections - 2 - stage
        ups = [
            tuple(jnp.where(mine, n, o) for n, o in zip(fresh[m], ups[m])) for m in range(micro)
        ]
    sums = [jnp.zeros(s, F32) for s in (square, square, (taps * width, LANES))]
    pieces = []
    for m in range(micro):
        part, up, *sums = back_pass(True, m, ups[m], sums)
        pieces += [up, part, swap(part)]

    grads = jnp.concatenate([s.astype(BF) for s in sums], axis=0)
    if spaces <= 4:
        copies = [grads] + [
            lax.ppermute(grads, "space", [(k, (k + d) % spaces) for k in range(spaces)])
            for d in range(1, spaces)
        ]
    else:
        copies = [lax.psum(grads, "space")]
    rows = grads.shape[0]
    out, exp_g, red_g, kg = pl.pallas_call(
        functools.partial(finish_kernel, micro, len(copies), scale),
        out_shape=[
            sds((micro,) + plane2, BF),
            sds(square, F32),
            sds(square, F32),
            sds((taps * width, LANES), F32),
        ],
        scratch_shapes=[pltpu.VMEM((len(copies), rows, LANES), BF)],
        name="finish",
        cost_estimate=cost(10**6, 4 * 2**20),
        compiler_params=params(),
    )(*pieces, *copies)
    kg = kg.reshape(taps, width, groups, width).transpose(0, 2, 1, 3)
    return (
        out.reshape(section_inputs.shape),
        exp_g[None],
        kg[None],
        red_g[None],
    )


def solution(mesh):
    placed = (
        P("section", "parts", "space", None, None, None),
        P("parts", "space", None, None, None),
        P("parts", "space", None, None),
        P("section", None, "chan"),
        P("section", None, "chan"),
        P("section", None, "chan", None, None),
        P("section", "chan", None),
    )
    return jax.shard_map(
        on_device,
        mesh=mesh,
        in_specs=placed,
        out_specs=(
            P("section", "parts", "space", None, None, None),
            P(("parts", "section"), None, "chan"),
            P(("parts", "section"), None, "chan", None, None),
            P(("parts", "section"), "chan", None),
        ),
        check_vma=False,
    )
```

```python
import functools
import math

import jax
import jax.numpy as jnp
from jax import lax
from jax.experimental import pallas as pl
from jax.experimental.pallas import tpu as pltpu
from jax.sharding import PartitionSpec as P

BF = jnp.bfloat16
F32 = jnp.float32
LANES = 128


def gate(v):
    return 0.5 + 0.5 * jnp.tanh(0.5 * v)


def slope(v, q):
    return q * (1.0 + v * (1.0 - q))


def nt_dot(a, b):
    return lax.dot_general(a, b, (((1,), (1,)), ((), ())), preferred_element_type=F32)


def store_shifts(ref, plane, value, wide, deep):
    cells = wide * deep
    cube = value.reshape(wide, deep, LANES)
    for j, turn in enumerate((1, 0, deep - 1)):
        moved = cube if turn == 0 else pltpu.roll(cube, turn, axis=1)
        flat = moved.reshape(cells, LANES).astype(BF)
        lanes = slice(j * LANES, (j + 1) * LANES)
        ref[plane, deep : deep + cells, lanes] = flat
        ref[plane, 0:deep, lanes] = flat[cells - deep :]
        ref[plane, deep + cells : cells + 2 * deep, lanes] = flat[:deep]


def views(ref, plane, cells, deep):
    return [
        ref[plane + dx, (1 + dy) * deep : (1 + dy) * deep + cells, :]
        for dx in (-1, 0, 1)
        for dy in (-1, 0, 1)
    ]


def conv_plane(ref, plane, weights, cells, deep):
    rows = jnp.concatenate(views(ref, plane, cells, deep), axis=1)
    return jnp.dot(rows, weights[...], preferred_element_type=F32)


def pack_kernel(micro, cells, wide, x_ref, ct_ref, lab_ref, *rest):
    outs, own_ref, sem = rest[: 2 * micro], rest[2 * micro], rest[2 * micro + 1]
    c = lax.axis_index("chan")
    copies = []
    for m in range(micro):
        a_ref, b_ref = outs[2 * m], outs[2 * m + 1]
        moves = (
            (x_ref.at[m, c], a_ref.at[0:cells]),
            (x_ref.at[m, c], b_ref.at[0:cells]),
            (ct_ref.at[m, c], a_ref.at[cells + wide : 2 * cells + wide]),
        )
        for n, (src, dst) in enumerate(moves):
            copy = pltpu.make_async_copy(src, dst, sem.at[3 * m + n])
            copy.start()
            copies.append(copy)
    deep = lab_ref.shape[3]
    row = lax.broadcasted_iota(jnp.int32, (LANES, LANES), 0)
    lane = lax.broadcasted_iota(jnp.int32, (LANES, LANES), 1)
    eye = jnp.where(row == lane, 1.0, 0.0)[:deep, :deep].astype(BF)
    for m in range(micro):
        for p in range(2):
            own_ref[m, p] = jnp.zeros((deep, LANES), BF)
            turned = nt_dot(eye, lab_ref[m, p].astype(F32).astype(BF))
            own_ref[m, p, :, 0:wide] = turned.astype(BF)
        lab = own_ref[m, c]
        outs[2 * m][cells : cells + wide] = lab
        outs[2 * m + 1][cells : cells + wide] = lab
    for copy in copies:
        copy.wait()


def diagonal_mask(width):
    groups = LANES // width
    g = lax.broadcasted_iota(jnp.int32, (groups, width, LANES), 0)
    lane = lax.broadcasted_iota(jnp.int32, (groups, width, LANES), 2)
    return g == lane // width


def weights_kernel(taps, width, k_ref, f_ref, b_ref, flat_ref, thin_ref):
    groups = LANES // width
    keep = diagonal_mask(width)
    flat_ref[:, 0:taps] = k_ref[...].astype(F32).reshape(groups * width * width, taps)
    for i in range(width):
        rows = [
            flat_ref[(g * width + i) * width : (g * width + i + 1) * width, :]
            for g in range(groups)
        ]
        turned = jnp.concatenate(rows, axis=0).T
        thin_ref[0, pl.ds(i, taps, stride=width), :] = turned[:taps]
        turned = flat_ref[pl.ds(i, LANES, stride=width), :].T
        thin_ref[1, pl.ds(i, taps, stride=width), :] = turned[:taps]
    for n, dst in enumerate((f_ref, b_ref)):
        for t in range(taps):
            one = thin_ref[n, t * width : (t + 1) * width, :]
            full = jnp.where(keep, jnp.broadcast_to(one[None], keep.shape), 0.0)
            at = t if n == 0 else taps - 1 - t
            dst[at * LANES : (at + 1) * LANES, :] = full.reshape(LANES, LANES).astype(BF)


def forward_kernel(
    wide,
    deep,
    x_ref,
    lab_ref,
    a_ref,
    b_ref,
    a2_ref,
    b2_ref,
    ct_ref,
    w_ref,
    code_ref,
    rw_ref,
    kf_ref,
    kb_ref,
    hid_ref,
    spre_ref,
    sconv_ref,
    mixed_ref,
    base_ref,
    other_ref,
    hs_ref,
    gs_ref,
    br_ref,
):
    c = lax.axis_index("chan")
    cells = wide * deep
    low, high = 1 - c, c
    codes = [jnp.broadcast_to(code_ref[i : i + 1, :], (deep, LANES)) for i in range(3)]

    def hidden_of(x, lab, plane, own):
        pre = jnp.dot(x, w_ref[...], preferred_element_type=F32)
        lab = lab.astype(F32)
        adds = []
        for y in range(wide):
            tag = jnp.broadcast_to(lab[:, y : y + 1], (deep, LANES))
            adds.append(jnp.where(tag < 0.5, codes[0], jnp.where(tag < 1.5, codes[1], codes[2])))
        pre = pre + jnp.concatenate(adds, axis=0)
        q = gate(pre)
        h = pre * q
        if own is not None:
            hid_ref[own] = h.astype(BF)
            spre_ref[own] = slope(pre, q)
        store_shifts(hs_ref, plane, h, wide, deep)

    hidden_of(x_ref[0, 0], lab_ref[0, 0], 2, 0)
    hidden_of(x_ref[0, 1], lab_ref[0, 1], 3, 1)
    for ref, plane in (
        (a_ref, 4 - 3 * c),
        (b_ref, 5 * c),
        (a2_ref, 1 + 3 * c),
        (b2_ref, 5 - 5 * c),
    ):
        hidden_of(ref[0:cells], ref[cells : cells + wide], plane, None)

    for p in range(4):
        conv = conv_plane(hs_ref, p + 1, kf_ref, cells, deep)
        q = gate(conv)
        sconv_ref[p] = slope(conv, q)
        if p in (1, 2):
            mixed_ref[p - 1] = (conv * q).astype(BF)

    ups = (
        (ct_ref[0, 0], 1),
        (ct_ref[0, 1], 2),
        (a_ref[cells + wide : 2 * cells + wide], 3 - 3 * c),
        (a2_ref[cells + wide : 2 * cells + wide], 3 * c),
    )
    for up, plane in ups:
        grad = nt_dot(up, rw_ref[...]) * sconv_ref[plane]
        store_shifts(gs_ref, plane, grad.astype(BF).astype(F32), wide, deep)
    for p in (0, 1):
        grad_hidden = conv_plane(gs_ref, p + 1, kb_ref, cells, deep)
        grad_pre = (grad_hidden * spre_ref[p]).astype(BF)
        br_ref[p] = nt_dot(grad_pre, w_ref[...])
    base_ref[...] = ct_ref[0, c].astype(F32) + br_ref[c]
    other_ref[...] = br_ref[1 - c].astype(BF)


def backward_kernel(
    full,
    wide,
    deep,
    taps,
    width,
    x_ref,
    ct_ref,
    cta_ref,
    cta2_ref,
    st_ref,
    st2_ref,
    dg_ref,
    dg2_ref,
    hid_ref,
    spre_ref,
    sconv_ref,
    mixed_ref,
    w_ref,
    rw_ref,
    kb_ref,
    *rest,
):
    c = lax.axis_index("chan")
    cells = wide * deep
    if full:
        exp_in, red_in, kg_in, part_ref, up_ref, exp_ref, red_ref, kg_ref, gs_ref = rest
    else:
        base_ref, other_ref, gs_ref, up_ref, br_ref = rest
    last = lax.axis_index("section") == lax.axis_size("section") - 1

    @pl.when(last)
    def _():
        up_ref[0] = ct_ref[0, 0]
        up_ref[1] = ct_ref[0, 1]

    @pl.when(jnp.logical_not(last))
    def _():
        up_ref[c] = st_ref[...]
        up_ref[1 - c] = st2_ref[...]

    tail = slice(cells + wide, 2 * cells + wide)
    halo = jnp.where(last, cta_ref[tail], dg_ref[...])
    halo2 = jnp.where(last, cta2_ref[tail], dg2_ref[...])
    ups = ((up_ref[0], 1), (up_ref[1], 2), (halo, 3 - 3 * c), (halo2, 3 * c))
    for up, plane in ups:
        grad = nt_dot(up, rw_ref[...]) * sconv_ref[plane]
        store_shifts(gs_ref, plane, grad.astype(BF).astype(F32), wide, deep)
    if full:
        ups2 = up_ref[...].reshape(2 * cells, LANES)
        red = lax.dot_general(
            mixed_ref[...].reshape(2 * cells, LANES),
            ups2,
            (((0,), (0,)), ((), ())),
            preferred_element_type=F32,
        )
        red_ref[...] = red_in[...] + red
        groups = LANES // width
        keep = diagonal_mask(width)
        turned = [hid_ref[p].T for p in (0, 1)]
        left = jnp.concatenate(turned, axis=1)
        for dx in (-1, 0, 1):
            for dy in (-1, 0, 1):
                rows = slice((1 + dy) * deep, (1 + dy) * deep + cells)
                right = jnp.concatenate([gs_ref[1 + dx, rows, :], gs_ref[2 + dx, rows, :]], axis=0)
                dense = jnp.dot(left, right, preferred_element_type=F32)
                for j in range(3):
                    tap = 9 * (dx + 1) + 3 * (dy + 1) + j
                    block = dense[:, j * LANES : (j + 1) * LANES].reshape(groups, width, LANES)
                    thin = jnp.sum(jnp.where(keep, block, 0.0), axis=0)
                    at = slice((taps - 1 - tap) * width, (taps - tap) * width)
                    kg_ref[at] = kg_in[at] + thin
    grads = []
    for p in (0, 1):
        grad_hidden = conv_plane(gs_ref, p + 1, kb_ref, cells, deep)
        grad_pre = (grad_hidden * spre_ref[p]).astype(BF)
        branch = nt_dot(grad_pre, w_ref[...])
        if full:
            part_ref[p] = branch.astype(BF)
            grads.append(grad_pre)
        else:
            br_ref[p] = branch
    if full:
        exp_ref[...] = exp_in[...] + lax.dot_general(
            x_ref[0].reshape(2 * cells, LANES),
            jnp.concatenate(grads, axis=0),
            (((0,), (0,)), ((), ())),
            preferred_element_type=F32,
        )
    else:
        base_ref[...] = up_ref[c].astype(F32) + br_ref[c]
        other_ref[...] = br_ref[1 - c].astype(BF)


def emit_kernel(micro, *refs):
    ins, out_ref = refs[:-1], refs[-1]
    for m in range(micro):
        up, mine, other = ins[3 * m : 3 * m + 3]
        both = mine[...].astype(F32) + other[...].astype(F32)
        out_ref[m] = (up[...].astype(F32) + both).astype(BF)


def finish_kernel(count, scale, taps, width, *refs):
    ins, outs, buf, thin_ref = refs[:count], refs[count:-2], refs[-2], refs[-1]
    rank = lax.axis_index("space")
    for d in range(count):
        buf[lax.rem(rank + count - d, count)] = ins[d][...]
    total = buf[0].astype(F32)
    for d in range(1, count):
        total = total + buf[d].astype(F32)
    total = total * scale
    outs[0][...] = total[0:LANES]
    outs[1][...] = total[LANES : 2 * LANES]
    thin_ref[0 : taps * width] = total[2 * LANES :]
    for i in range(width):
        turned = thin_ref[pl.ds(i, LANES, stride=width), :].T
        outs[2][:, i] = turned[:, :taps].reshape(LANES // width, width, taps)


def sds(shape, dtype):
    return jax.ShapeDtypeStruct(shape, dtype)


def params():
    return pltpu.CompilerParams(vmem_limit_bytes=40 * 2**20)


def cost(flops, nbytes):
    return pl.CostEstimate(flops=flops, bytes_accessed=nbytes, transcendentals=0)


def whole(shape):
    return pl.BlockSpec(shape, lambda i: (0,) * len(shape))


def picked(shape, m):
    return pl.BlockSpec((1,) + shape, lambda i: (m,) + (0,) * len(shape))


def on_device(
    section_inputs, cotangent, phase_labels, expand_weight, phase_code, kernel, reduce_weight
):
    _, micro, depth, wide, deep, trunk = section_inputs.shape
    cells = wide * deep
    taps, groups, width = kernel.shape[1], kernel.shape[2], kernel.shape[3]
    assert depth == 2 and lax.axis_size("chan") == 2
    assert trunk == LANES and groups * width == LANES
    spaces, sections = lax.axis_size("space"), lax.axis_size("section")
    scale = 1.0 / math.sqrt(micro * depth * spaces * cells)

    x = section_inputs[0].reshape(micro, depth, cells, trunk)
    ct = cotangent.reshape(micro, depth, cells, trunk)
    w, rw = expand_weight[0], reduce_weight[0]
    code = jnp.pad(phase_code[0], ((0, 8 - phase_code.shape[1]), (0, 0)))
    kern = kernel[0].transpose(1, 2, 3, 0)

    away = [(k, c, (k + 2 * c - 1) % spaces) for k in range(spaces) for c in (0, 1)]
    back = [(k, c, (k - 2 * c + 1) % spaces) for k in range(spaces) for c in (0, 1)]
    route_a = [(2 * k + c, 2 * t + c) for k, c, t in away]
    route_b = [(2 * k + c, 2 * t + c) for k, c, t in back]
    route_d = [
        ((k * sections + s) * 2 + c, (t * sections + (s - 1) % sections) * 2 + c)
        for k, c, t in away
        for s in range(sections)
    ]
    route_s = [(s, (s - 1) % sections) for s in range(sections)]

    def swap(v):
        return lax.ppermute(v, "chan", [(0, 1), (1, 0)])

    rows_a, rows_b = 2 * cells + wide, cells + wide
    hbm = pl.BlockSpec(memory_space=pl.ANY)
    vmem = pl.BlockSpec(memory_space=pltpu.VMEM)
    *packed, lab = pl.pallas_call(
        functools.partial(pack_kernel, micro, cells, wide),
        in_specs=[hbm, hbm, vmem],
        out_specs=[vmem] * (2 * micro + 1),
        out_shape=[sds((n, LANES), BF) for _ in range(micro) for n in (rows_a, rows_b)]
        + [sds((micro, depth, deep, LANES), BF)],
        scratch_shapes=[pltpu.SemaphoreType.DMA((3 * micro,))],
        name="pack",
        cost_estimate=cost(0, 4 * 2**20),
        compiler_params=params(),
    )(x, ct, phase_labels)
    dense_f, dense_b = pl.pallas_call(
        functools.partial(weights_kernel, taps, width),
        out_shape=[sds((taps * LANES, LANES), BF)] * 2,
        scratch_shapes=[
            pltpu.VMEM((LANES * width, LANES), F32),
            pltpu.VMEM((2, taps * width, LANES), F32),
        ],
        name="weights",
        cost_estimate=cost(0, 2 * 2**20),
        compiler_params=params(),
    )(kern)
    halos = []
    for m in range(micro):
        a = lax.ppermute(packed[2 * m], ("space", "chan"), route_a)
        b = lax.ppermute(packed[2 * m + 1], ("space", "chan"), route_b)
        if m == 0:
            a, b, dense_f, dense_b = lax.optimization_barrier((a, b, dense_f, dense_b))
        halos.append((a, b, swap(a), swap(b)))

    plane2, plane4 = (2, cells, LANES), (4, cells, LANES)
    pad_rows = cells + 2 * deep
    shape_a, shape_b = (2 * cells + wide, LANES), (cells + wide, LANES)
    square, tall = (LANES, LANES), (taps * LANES, LANES)
    saved, ups, waiting = [], [], []

    def joined(base, other):
        return (base + swap(other).astype(F32)).astype(BF)

    def send_on(out):
        st = lax.ppermute(out, "section", route_s)
        dg = lax.ppermute(out, ("space", "section", "chan"), route_d)
        return st, swap(st), dg, swap(dg)

    for m in range(micro):
        a, b, a2, b2 = halos[m]
        if m >= 2:
            out = joined(*waiting.pop(0))
            out, code = lax.optimization_barrier((out, code))
            ups.append(send_on(out))
        hid, spre, sconv, mixed, base, other = pl.pallas_call(
            functools.partial(forward_kernel, wide, deep),
            grid=(1,),
            in_specs=[
                picked(plane2, m),
                picked((2, deep, LANES), m),
                whole(shape_a),
                whole(shape_b),
                whole(shape_a),
                whole(shape_b),
                picked(plane2, m),
                whole(square),
                whole((8, LANES)),
                whole(square),
                whole(tall),
                whole(tall),
            ],
            out_specs=[
                whole(plane2),
                whole(plane2),
                whole(plane4),
                whole(plane2),
                whole((cells, LANES)),
                whole((cells, LANES)),
            ],
            out_shape=[
                sds(plane2, BF),
                sds(plane2, F32),
                sds(plane4, F32),
                sds(plane2, BF),
                sds((cells, LANES), F32),
                sds((cells, LANES), BF),
            ],
            scratch_shapes=[
                pltpu.VMEM((6, pad_rows, 3 * LANES), BF),
                pltpu.VMEM((4, pad_rows, 3 * LANES), BF),
                pltpu.VMEM(plane2, F32),
            ],
            name="forward",
            cost_estimate=cost(2 * 10**9, 5 * 2**20),
            compiler_params=params(),
        )(x, lab, a, b, a2, b2, ct, w, code, rw, dense_f, dense_b)
        saved.append((hid, spre, sconv, mixed))
        waiting.append((base, other))
    ups += [send_on(joined(*pair)) for pair in waiting]

    def back_pass(full, m, ups, sums):
        hid, spre, sconv, mixed = saved[m]
        a, _, a2, _ = halos[m]
        st, st2, dg, dg2 = ups
        flat = (cells, LANES)
        in_specs = [
            picked(plane2, m),
            picked(plane2, m),
            whole(shape_a),
            whole(shape_a),
            whole(flat),
            whole(flat),
            whole(flat),
            whole(flat),
            whole(plane2),
            whole(plane2),
            whole(plane4),
            whole(plane2),
            whole(square),
            whole(square),
            whole(tall),
        ]
        scratch = [pltpu.VMEM((4, pad_rows, 3 * LANES), BF)]
        sum_shapes = [square, square, (taps * width, LANES)]
        if full:
            out_shape = [sds(plane2, BF), sds(plane2, BF)] + [sds(s, F32) for s in sum_shapes]
            in_specs = in_specs + [whole(s) for s in sum_shapes]
        else:
            out_shape = [sds(flat, F32), sds(flat, BF)]
            scratch = scratch + [pltpu.VMEM(plane2, BF), pltpu.VMEM(plane2, F32)]
        return pl.pallas_call(
            functools.partial(backward_kernel, full, wide, deep, taps, width),
            grid=(1,),
            in_specs=in_specs,
            out_specs=[whole(s.shape) for s in out_shape],
            out_shape=out_shape,
            scratch_shapes=scratch,
            name="backward" if full else "backward_light",
            cost_estimate=cost(2 * 10**9, 5 * 2**20),
            compiler_params=params(),
        )(x, ct, a, a2, st, st2, dg, dg2, hid, spre, sconv, mixed, w, rw, dense_b, *sums)

    rank = lax.axis_index("section")
    for stage in range(1, sections - 1):
        fresh = [send_on(joined(*back_pass(False, m, ups[m], ()))) for m in range(micro)]
        mine = rank == sections - 2 - stage
        ups = [
            tuple(jnp.where(mine, n, o) for n, o in zip(fresh[m], ups[m])) for m in range(micro)
        ]
    sums = [jnp.zeros(s, F32) for s in (square, square, (taps * width, LANES))]
    pieces = []
    for m in range(micro):
        part, up, *sums = back_pass(True, m, ups[m], sums)
        pieces += [up, part, swap(part)]

    grads = jnp.concatenate([s.astype(BF) for s in sums], axis=0)
    if spaces <= 4:
        copies = [grads] + [
            lax.ppermute(grads, "space", [(k, (k + d) % spaces) for k in range(spaces)])
            for d in range(1, spaces)
        ]
    else:
        copies = [lax.psum(grads, "space")]
    out = pl.pallas_call(
        functools.partial(emit_kernel, micro),
        out_shape=sds((micro,) + plane2, BF),
        name="emit",
        cost_estimate=cost(10**6, 4 * 2**20),
        compiler_params=params(),
    )(*pieces)
    exp_g, red_g, kg = pl.pallas_call(
        functools.partial(finish_kernel, len(copies), scale, taps, width),
        out_shape=[
            sds(square, F32),
            sds(square, F32),
            sds((groups, width, width, taps), F32),
        ],
        scratch_shapes=[
            pltpu.VMEM((len(copies),) + grads.shape, BF),
            pltpu.VMEM((LANES * width, LANES), F32),
        ],
        name="finish",
        cost_estimate=cost(10**6, 4 * 2**20),
        compiler_params=params(),
    )(*copies)
    kg = kg.transpose(3, 0, 1, 2)
    return (
        out.reshape(section_inputs.shape),
        exp_g[None],
        kg[None],
        red_g[None],
    )


def solution(mesh):
    placed = (
        P("section", "parts", "space", None, None, None),
        P("parts", "space", None, None, None),
        P("parts", "space", None, None),
        P("section", None, "chan"),
        P("section", None, "chan"),
        P("section", None, "chan", None, None),
        P("section", "chan", None),
    )
    return jax.shard_map(
        on_device,
        mesh=mesh,
        in_specs=placed,
        out_specs=(
            P("section", "parts", "space", None, None, None),
            P(("parts", "section"), None, "chan"),
            P(("parts", "section"), None, "chan", None, None),
            P(("parts", "section"), "chan", None),
        ),
        check_vma=False,
    )
```

```python
import functools
import math

import jax
import jax.numpy as jnp
from jax import lax
from jax.experimental import pallas as pl
from jax.experimental.pallas import tpu as pltpu
from jax.sharding import PartitionSpec as P

BF = jnp.bfloat16
F32 = jnp.float32
LANES = 128


def gate(v):
    return 0.5 + 0.5 * jnp.tanh(0.5 * v)


def slope(v, q):
    return q * (1.0 + v * (1.0 - q))


def nt_dot(a, b):
    return lax.dot_general(a, b, (((1,), (1,)), ((), ())), preferred_element_type=F32)


def store_shifts(ref, plane, value, wide, deep):
    cells = wide * deep
    cube = value.reshape(wide, deep, LANES)
    for j, turn in enumerate((1, 0, deep - 1)):
        moved = cube if turn == 0 else pltpu.roll(cube, turn, axis=1)
        flat = moved.reshape(cells, LANES).astype(BF)
        lanes = slice(j * LANES, (j + 1) * LANES)
        ref[plane, deep : deep + cells, lanes] = flat
        ref[plane, 0:deep, lanes] = flat[cells - deep :]
        ref[plane, deep + cells : cells + 2 * deep, lanes] = flat[:deep]


def pair_rows(planes, first, cells, deep):
    parts = []
    for at in range(first - 1, first + 3):
        ref, plane = planes[at]
        for dy in range(3):
            parts.append(ref[plane, dy * deep : dy * deep + cells, :])
    return jnp.concatenate(parts, axis=1)


def conv_pairs(planes, firsts, weights, cells, deep):
    rows = [pair_rows(planes, first, cells, deep) for first in firsts]
    rows = rows[0] if len(rows) == 1 else jnp.concatenate(rows, axis=0)
    both = jnp.dot(rows, weights[...], preferred_element_type=F32)
    outs = []
    for n in range(len(firsts)):
        for o in range(2):
            outs.append(both[n * cells : (n + 1) * cells, o * LANES : (o + 1) * LANES])
    return outs


def pack_kernel(groups, cells, wide, x_ref, ct_ref, tag_ref, *rest):
    micro = sum(len(group) for group in groups)
    outs, (own_ref, lab_ref, sem) = rest[: 2 * len(groups)], rest[2 * len(groups) :]
    spots = []
    for n, group in enumerate(groups):
        for i in range(len(group)):
            at = i * (cells + wide)
            a_ref = outs[2 * n].at[pl.ds(at + i * cells, 2 * cells + wide)]
            spots.append((a_ref, outs[2 * n + 1].at[pl.ds(at, cells + wide)]))
    tags = pltpu.make_async_copy(tag_ref, lab_ref, sem.at[3 * micro])
    tags.start()
    c = lax.axis_index("chan")
    copies = []
    for m in range(micro):
        a_ref, b_ref = spots[m]
        moves = (
            (x_ref.at[m, c], a_ref.at[0:cells]),
            (x_ref.at[m, c], b_ref.at[0:cells]),
            (ct_ref.at[m, c], a_ref.at[cells + wide : 2 * cells + wide]),
        )
        for n, (src, dst) in enumerate(moves):
            copy = pltpu.make_async_copy(src, dst, sem.at[3 * m + n])
            copy.start()
            copies.append(copy)
    deep = lab_ref.shape[3]
    tags.wait()
    row = lax.broadcasted_iota(jnp.int32, (LANES, LANES), 0)
    lane = lax.broadcasted_iota(jnp.int32, (LANES, LANES), 1)
    eye = jnp.where(row == lane, 1.0, 0.0)[:deep, :deep].astype(BF)
    for m in range(micro):
        for p in range(2):
            own_ref[m, p] = jnp.zeros((deep, LANES), BF)
            turned = nt_dot(eye, lab_ref[m, p].astype(F32).astype(BF))
            own_ref[m, p, :, 0:wide] = turned.astype(BF)
        lab = own_ref[m, c]
        spots[m][0][cells : cells + wide] = lab
        spots[m][1][cells : cells + wide] = lab
    for copy in copies:
        copy.wait()


def diagonal_mask(width):
    groups = LANES // width
    g = lax.broadcasted_iota(jnp.int32, (groups, width, LANES), 0)
    lane = lax.broadcasted_iota(jnp.int32, (groups, width, LANES), 2)
    return g == lane // width


def weights_kernel(taps, width, k_ref, f_ref, b_ref, flat_ref, thin_ref):
    groups = LANES // width
    keep = diagonal_mask(width)
    flat_ref[:, 0:taps] = k_ref[...].astype(F32).reshape(groups * width * width, taps)
    for i in range(width):
        rows = [
            flat_ref[(g * width + i) * width : (g * width + i + 1) * width, :]
            for g in range(groups)
        ]
        turned = jnp.concatenate(rows, axis=0).T
        thin_ref[0, pl.ds(i, taps, stride=width), :] = turned[:taps]
        turned = flat_ref[pl.ds(i, LANES, stride=width), :].T
        thin_ref[1, pl.ds(i, taps, stride=width), :] = turned[:taps]
    third = taps // 3 * LANES
    zero = jnp.zeros((third, LANES), BF)
    for n, dst in enumerate((f_ref, b_ref)):
        dst[0:third, LANES:] = zero
        dst[3 * third :, 0:LANES] = zero
        for t in range(taps):
            one = thin_ref[n, t * width : (t + 1) * width, :]
            full = jnp.where(keep, jnp.broadcast_to(one[None], keep.shape), 0.0)
            full = full.reshape(LANES, LANES).astype(BF)
            at = (t if n == 0 else taps - 1 - t) * LANES
            dst[at : at + LANES, 0:LANES] = full
            dst[third + at : third + at + LANES, LANES:] = full


def hidden_rows(x, lab, w, codes, wide, deep):
    pre = jnp.dot(x, w, preferred_element_type=F32)
    lab = lab.astype(F32)
    adds = []
    for y in range(wide):
        tag = jnp.broadcast_to(lab[:, y : y + 1], (deep, LANES))
        adds.append(jnp.where(tag < 0.5, codes[0], jnp.where(tag < 1.5, codes[1], codes[2])))
    return pre + jnp.concatenate(adds, axis=0)


def code_rows(code_ref, deep):
    return [jnp.broadcast_to(code_ref[i : i + 1, :], (deep, LANES)) for i in range(3)]


def own_kernel(
    micro, wide, deep, x_ref, ct_ref, lab_ref, w_ref, rw_ref, code_ref, *outs
):
    for src, dst in zip((x_ref, ct_ref, w_ref, rw_ref, code_ref), outs[3 * micro :]):
        dst[...] = src[...]
    codes = code_rows(code_ref, deep)
    for m in range(micro):
        hs_ref, hid_ref, spre_ref = outs[3 * m : 3 * m + 3]
        for p in range(2):
            pre = hidden_rows(x_ref[m, p], lab_ref[m, p], w_ref[...], codes, wide, deep)
            q = gate(pre)
            h = pre * q
            hid_ref[p] = h.astype(BF)
            spre_ref[p] = slope(pre, q)
            store_shifts(hs_ref, p, h, wide, deep)


def forward_kernel(
    slot,
    wide,
    deep,
    own_ref,
    a_ref,
    b_ref,
    a2_ref,
    b2_ref,
    w_ref,
    code_ref,
    kf_ref,
    sconv_ref,
    mixed_ref,
    hs_ref,
):
    c = lax.axis_index("chan")
    cells = wide * deep
    codes = code_rows(code_ref, deep)
    a_ref, a2_ref = [v.at[pl.ds(slot * (2 * cells + wide), 2 * cells + wide)] for v in (a_ref, a2_ref)]
    b_ref, b2_ref = [v.at[pl.ds(slot * (cells + wide), cells + wide)] for v in (b_ref, b2_ref)]
    for ref, plane in ((a_ref, 2 - c), (b_ref, 3 * c), (a2_ref, 1 + c), (b2_ref, 3 - 3 * c)):
        lab = ref[cells : cells + wide]
        pre = hidden_rows(ref[0:cells], lab, w_ref[...], codes, wide, deep)
        store_shifts(hs_ref, plane, pre * gate(pre), wide, deep)
    planes = [(hs_ref, 0), (hs_ref, 1), (own_ref, 0), (own_ref, 1), (hs_ref, 2), (hs_ref, 3)]
    for p, conv in enumerate(conv_pairs(planes, (1, 3), kf_ref, cells, deep)):
        q = gate(conv)
        sconv_ref[p] = slope(conv, q)
        if p in (1, 2):
            mixed_ref[p - 1] = (conv * q).astype(BF)


def backward_kernel(
    mode,
    m,
    slot,
    wide,
    deep,
    taps,
    width,
    x_ref,
    ct_ref,
    cta_ref,
    cta2_ref,
    w_ref,
    rw_ref,
    kb_ref,
    spre_ref,
    sconv_ref,
    *rest,
):
    c = lax.axis_index("chan")
    cells = wide * deep
    tail = pl.ds(slot * (2 * cells + wide) + cells + wide, cells)
    full = mode == "full"
    if mode == "first":
        base_ref, other_ref, gs_ref, br_ref = rest
        up_ref = ct_ref.at[m]
        halo, halo2 = cta_ref[tail], cta2_ref[tail]
    else:
        st_ref, st2_ref, dg_ref, dg2_ref, *rest = rest
        if full:
            hid_ref, mixed_ref, exp_in, red_in, kg_in, *rest = rest
            part_ref, up_ref, exp_ref, red_ref, kg_ref, gs_ref = rest
        else:
            base_ref, other_ref, gs_ref, br_ref, up_ref = rest
        last = lax.axis_index("section") == lax.axis_size("section") - 1

        @pl.when(last)
        def _():
            up_ref[0] = ct_ref[m, 0]
            up_ref[1] = ct_ref[m, 1]

        @pl.when(jnp.logical_not(last))
        def _():
            up_ref[c] = st_ref[...]
            up_ref[1 - c] = st2_ref[...]

        halo = jnp.where(last, cta_ref[tail], dg_ref[...])
        halo2 = jnp.where(last, cta2_ref[tail], dg2_ref[...])
    ups = ((up_ref[0], 1), (up_ref[1], 2), (halo, 3 - 3 * c), (halo2, 3 * c))
    for up, plane in ups:
        grad = nt_dot(up, rw_ref[...]) * sconv_ref[plane]
        store_shifts(gs_ref, plane, grad.astype(BF).astype(F32), wide, deep)
    if full:
        ups2 = up_ref[...].reshape(2 * cells, LANES)
        red = lax.dot_general(
            mixed_ref[...].reshape(2 * cells, LANES),
            ups2,
            (((0,), (0,)), ((), ())),
            preferred_element_type=F32,
        )
        red_ref[...] = red_in[...] + red
        groups = LANES // width
        keep = diagonal_mask(width)
        turned = [hid_ref[p].T for p in (0, 1)]
        left = jnp.concatenate(turned, axis=1)
        for dx in (-1, 0, 1):
            for dy in (-1, 0, 1):
                rows = slice((1 + dy) * deep, (1 + dy) * deep + cells)
                right = jnp.concatenate([gs_ref[1 + dx, rows, :], gs_ref[2 + dx, rows, :]], axis=0)
                dense = jnp.dot(left, right, preferred_element_type=F32)
                for j in range(3):
                    tap = 9 * (dx + 1) + 3 * (dy + 1) + j
                    block = dense[:, j * LANES : (j + 1) * LANES].reshape(groups, width, LANES)
                    thin = jnp.sum(jnp.where(keep, block, 0.0), axis=0)
                    at = slice((taps - 1 - tap) * width, (taps - tap) * width)
                    kg_ref[at] = kg_in[at] + thin
    planes = [(gs_ref, p) for p in range(4)]
    grads = []
    for p, grad_hidden in enumerate(conv_pairs(planes, (1,), kb_ref, cells, deep)):
        grad_pre = (grad_hidden * spre_ref[p]).astype(BF)
        branch = nt_dot(grad_pre, w_ref[...])
        if full:
            part_ref[p] = branch.astype(BF)
            grads.append(grad_pre)
        else:
            br_ref[p] = branch
    if full:
        exp_ref[...] = exp_in[...] + lax.dot_general(
            x_ref[m].reshape(2 * cells, LANES),
            jnp.concatenate(grads, axis=0),
            (((0,), (0,)), ((), ())),
            preferred_element_type=F32,
        )
    else:
        base_ref[...] = up_ref[c].astype(F32) + br_ref[c]
        other_ref[...] = br_ref[1 - c].astype(BF)


def emit_kernel(micro, *refs):
    ins, out_ref = refs[:-1], refs[-1]
    for m in range(micro):
        up, mine, other = ins[3 * m : 3 * m + 3]
        both = mine[...].astype(F32) + other[...].astype(F32)
        out_ref[m] = (up[...].astype(F32) + both).astype(BF)


def finish_kernel(count, scale, taps, width, *refs):
    ins, outs, thin_ref = refs[:count], refs[count:-1], refs[-1]
    total = ins[0][...].astype(F32)
    for ref in ins[1:]:
        total = total + ref[...].astype(F32)
    total = total * scale
    outs[0][...] = total[0:LANES]
    outs[1][...] = total[LANES : 2 * LANES]
    thin_ref[0 : taps * width] = total[2 * LANES :]
    for i in range(width):
        turned = thin_ref[pl.ds(i, LANES, stride=width), :].T
        outs[2][:, i] = turned[:, :taps].reshape(LANES // width, width, taps)


def GROUPS(micro):
    return [list(range(micro))]


def sds(shape, dtype):
    return jax.ShapeDtypeStruct(shape, dtype)


def params(mebibytes):
    return pltpu.CompilerParams(vmem_limit_bytes=mebibytes * 2**20)


def call(kernel, name, out_shape, args, scratch=(), in_specs=None, room=16):
    vmem = pl.BlockSpec(memory_space=pltpu.VMEM)
    outs = [vmem] * len(out_shape)
    return pl.pallas_call(
        kernel,
        in_specs=[vmem] * len(args) if in_specs is None else in_specs,
        out_specs=outs,
        out_shape=out_shape,
        scratch_shapes=list(scratch),
        name=name,
        cost_estimate=pl.CostEstimate(flops=1000, bytes_accessed=1000, transcendentals=0),
        compiler_params=params(room),
    )(*args)


def on_device(
    section_inputs, cotangent, phase_labels, expand_weight, phase_code, kernel, reduce_weight
):
    _, micro, depth, wide, deep, trunk = section_inputs.shape
    cells = wide * deep
    taps, groups, width = kernel.shape[1], kernel.shape[2], kernel.shape[3]
    assert depth == 2 and lax.axis_size("chan") == 2
    assert trunk == LANES and groups * width == LANES
    spaces, sections = lax.axis_size("space"), lax.axis_size("section")
    scale = 1.0 / math.sqrt(micro * depth * spaces * cells)

    x = section_inputs[0].reshape(micro, depth, cells, trunk)
    ct = cotangent.reshape(micro, depth, cells, trunk)
    w, rw = expand_weight[0], reduce_weight[0]
    code = jnp.pad(phase_code[0], ((0, 8 - phase_code.shape[1]), (0, 0)))
    kern = kernel[0].transpose(1, 2, 3, 0)

    away = [(k, c, (k + 2 * c - 1) % spaces) for k in range(spaces) for c in (0, 1)]
    back = [(k, c, (k - 2 * c + 1) % spaces) for k in range(spaces) for c in (0, 1)]
    route_a = [(2 * k + c, 2 * t + c) for k, c, t in away]
    route_b = [(2 * k + c, 2 * t + c) for k, c, t in back]
    route_d = [
        ((k * sections + s) * 2 + c, (t * sections + (s - 1) % sections) * 2 + c)
        for k, c, t in away
        for s in range(sections)
    ]
    route_s = [(s, (s - 1) % sections) for s in range(sections)]

    def swap(v):
        return lax.ppermute(v, "chan", [(0, 1), (1, 0)])

    groups_m = GROUPS(micro)
    rows_a, rows_b = 2 * cells + wide, cells + wide
    hbm = pl.BlockSpec(memory_space=pltpu.HBM)
    *packed, lab = call(
        functools.partial(pack_kernel, groups_m, cells, wide),
        "pack",
        [sds((len(g) * n, LANES), BF) for g in groups_m for n in (rows_a, rows_b)]
        + [sds((micro, depth, deep, LANES), BF)],
        (x, ct, phase_labels),
        [
            pltpu.VMEM(phase_labels.shape, jnp.int32),
            pltpu.SemaphoreType.DMA((3 * micro + 1,)),
        ],
        [hbm, hbm, hbm],
        60,
    )
    plane2, plane4, flat = (2, cells, LANES), (4, cells, LANES), (cells, LANES)
    pad_rows = cells + 2 * deep
    square, thin = (LANES, LANES), (taps * width, LANES)
    dense_f, dense_b = call(
        functools.partial(weights_kernel, taps, width),
        "weights",
        [sds((4 * taps // 3 * LANES, 2 * LANES), BF)] * 2,
        (kern,),
        [pltpu.VMEM((LANES * width, LANES), F32), pltpu.VMEM((2,) + thin, F32)],
    )
    *owned, x, ct, w, rw, code = call(
        functools.partial(own_kernel, micro, wide, deep),
        "own",
        [sds((2, pad_rows, 3 * LANES), BF), sds(plane2, BF), sds(plane2, F32)] * micro
        + [sds(v.shape, v.dtype) for v in (x, ct, w, rw, code)],
        (x, ct, lab, w, rw, code),
    )
    halos, slots = [], []
    for n, group in enumerate(groups_m):
        a = lax.ppermute(packed[2 * n], ("space", "chan"), route_a)
        b = lax.ppermute(packed[2 * n + 1], ("space", "chan"), route_b)
        if n == 0:
            a, b, dense_f, dense_b, *owned = lax.optimization_barrier(
                (a, b, dense_f, dense_b, *owned)
            )
        halos += [(a, b, swap(a), swap(b))] * len(group)
        slots += list(range(len(group)))

    def joined(base, other):
        return (base + swap(other).astype(F32)).astype(BF)

    def send_on(out):
        st = lax.ppermute(out, "section", route_s)
        dg = lax.ppermute(out, ("space", "section", "chan"), route_d)
        return st, swap(st), dg, swap(dg)

    def back_pass(mode, m, extra, extra_out=()):
        outs = [sds(flat, F32), sds(flat, BF)] if mode != "full" else [sds(plane2, BF)] * 2
        scratch = [pltpu.VMEM((4, pad_rows, 3 * LANES), BF)]
        if mode != "full":
            scratch.append(pltpu.VMEM(plane2, F32))
        if mode == "light":
            scratch.append(pltpu.VMEM(plane2, BF))
        return call(
            functools.partial(backward_kernel, mode, m, slots[m], wide, deep, taps, width),
            "backward_" + mode,
            outs + list(extra_out),
            (x, ct, halos[m][0], halos[m][2], w, rw, dense_b, spre[m], sconv[m], *extra),
            scratch,
        )

    sconv, mixed, ups = [], [], []
    spre = [owned[3 * m + 2] for m in range(micro)]
    pending = None
    for m in range(micro):
        a, b, a2, b2 = halos[m]
        con, mix = call(
            functools.partial(forward_kernel, slots[m], wide, deep),
            "forward",
            [sds(plane4, F32), sds(plane2, BF)],
            (owned[3 * m], a, b, a2, b2, w, code, dense_f),
            [pltpu.VMEM((4, pad_rows, 3 * LANES), BF)],
        )
        sconv.append(con)
        mixed.append(mix)
        if pending is not None:
            out, sconv[m] = lax.optimization_barrier((joined(*pending), sconv[m]))
            ups.append(send_on(out))
        pending = back_pass("first", m, ())
    ups.append(send_on(joined(*pending)))

    rank = lax.axis_index("section")
    for stage in range(1, sections - 1):
        fresh = [send_on(joined(*back_pass("light", m, ups[m]))) for m in range(micro)]
        mine = rank == sections - 2 - stage
        ups = [
            tuple(jnp.where(mine, n, o) for n, o in zip(fresh[m], ups[m])) for m in range(micro)
        ]
    sum_shapes = [sds(s, F32) for s in (square, square, thin)]
    sums = [jnp.zeros(s.shape, F32) for s in sum_shapes]
    pieces = []
    for m in range(micro):
        extra = (*ups[m], owned[3 * m + 1], mixed[m], *sums)
        part, up, *sums = back_pass("full", m, extra, sum_shapes)
        pieces += [up, part, swap(part)]

    grads = jnp.concatenate([s.astype(BF) for s in sums], axis=0)
    if spaces == 4:
        near = [(k, k ^ 1) for k in range(spaces)]
        far = [(k, k ^ 3) for k in range(spaces)]
        grads = grads + lax.ppermute(grads, "space", near)
        copies = [grads, lax.ppermute(grads, "space", far)]
    else:
        copies = [lax.psum(grads, "space")]
    (out,) = call(
        functools.partial(emit_kernel, micro), "emit", [sds((micro,) + plane2, BF)], pieces
    )
    *copies, out = lax.optimization_barrier((*copies, out))
    exp_g, red_g, kg = call(
        functools.partial(finish_kernel, len(copies), scale, taps, width),
        "finish",
        [sds(square, F32), sds(square, F32), sds((groups, width, width, taps), F32)],
        copies,
        [pltpu.VMEM((LANES * width, LANES), F32)],
    )
    kg = kg.transpose(3, 0, 1, 2)
    return (
        out.reshape(section_inputs.shape),
        exp_g[None],
        kg[None],
        red_g[None],
    )


def solution(mesh):
    placed = (
        P("section", "parts", "space", None, None, None),
        P("parts", "space", None, None, None),
        P("parts", "space", None, None),
        P("section", None, "chan"),
        P("section", None, "chan"),
        P("section", None, "chan", None, None),
        P("section", "chan", None),
    )
    return jax.shard_map(
        on_device,
        mesh=mesh,
        in_specs=placed,
        out_specs=(
            P("section", "parts", "space", None, None, None),
            P(("parts", "section"), None, "chan"),
            P(("parts", "section"), None, "chan", None, None),
            P(("parts", "section"), "chan", None),
        ),
        check_vma=False,
    )
```

```python
import functools
import math

import jax
import jax.numpy as jnp
from jax import lax
from jax.experimental import pallas as pl
from jax.experimental.pallas import tpu as pltpu
from jax.sharding import PartitionSpec as P

BF = jnp.bfloat16
F32 = jnp.float32
LANES = 128


def gate(v):
    return 0.5 + 0.5 * jnp.tanh(0.5 * v)


def slope(v, q):
    return q * (1.0 + v * (1.0 - q))


def nt_dot(a, b):
    return lax.dot_general(a, b, (((1,), (1,)), ((), ())), preferred_element_type=F32)


def store_shifts(ref, plane, value, wide, deep):
    cells = wide * deep
    cube = value.reshape(wide, deep, LANES)
    for j, turn in enumerate((1, 0, deep - 1)):
        moved = cube if turn == 0 else pltpu.roll(cube, turn, axis=1)
        flat = moved.reshape(cells, LANES).astype(BF)
        lanes = slice(j * LANES, (j + 1) * LANES)
        ref[plane, deep : deep + cells, lanes] = flat
        ref[plane, 0:deep, lanes] = flat[cells - deep :]
        ref[plane, deep + cells : cells + 2 * deep, lanes] = flat[:deep]


def pair_rows(planes, first, cells, deep):
    parts = []
    for at in range(first - 1, first + 3):
        ref, plane = planes[at]
        for dy in range(3):
            parts.append(ref[plane, dy * deep : dy * deep + cells, :])
    return jnp.concatenate(parts, axis=1)


def conv_pairs(planes, firsts, weights, cells, deep):
    rows = [pair_rows(planes, first, cells, deep) for first in firsts]
    rows = rows[0] if len(rows) == 1 else jnp.concatenate(rows, axis=0)
    both = jnp.dot(rows, weights[...], preferred_element_type=F32)
    outs = []
    for n in range(len(firsts)):
        for o in range(2):
            outs.append(both[n * cells : (n + 1) * cells, o * LANES : (o + 1) * LANES])
    return outs


def pack_kernel(micro, cells, wide, x_ref, tag_ref, out_ref, own_ref, lab_ref, sem):
    tags = pltpu.make_async_copy(tag_ref, lab_ref, sem.at[micro])
    tags.start()
    c = lax.axis_index("chan")
    copies = []
    for m in range(micro):
        spot = out_ref.at[pl.ds(m * (cells + wide), cells)]
        copy = pltpu.make_async_copy(x_ref.at[m, c], spot, sem.at[m])
        copy.start()
        copies.append(copy)
    deep = lab_ref.shape[3]
    tags.wait()
    row = lax.broadcasted_iota(jnp.int32, (LANES, LANES), 0)
    lane = lax.broadcasted_iota(jnp.int32, (LANES, LANES), 1)
    eye = jnp.where(row == lane, 1.0, 0.0)[:deep, :deep].astype(BF)
    for m in range(micro):
        for p in range(2):
            own_ref[m, p] = jnp.zeros((deep, LANES), BF)
            turned = nt_dot(eye, lab_ref[m, p].astype(F32).astype(BF))
            own_ref[m, p, :, 0:wide] = turned.astype(BF)
        out_ref[m * (cells + wide) + cells : (m + 1) * (cells + wide)] = own_ref[m, c]
    for copy in copies:
        copy.wait()


def diagonal_mask(width):
    groups = LANES // width
    g = lax.broadcasted_iota(jnp.int32, (groups, width, LANES), 0)
    lane = lax.broadcasted_iota(jnp.int32, (groups, width, LANES), 2)
    return g == lane // width


def weights_kernel(taps, width, k_ref, f_ref, b_ref, flat_ref, thin_ref):
    groups = LANES // width
    keep = diagonal_mask(width)
    flat_ref[:, 0:taps] = k_ref[...].astype(F32).reshape(groups * width * width, taps)
    for i in range(width):
        rows = [
            flat_ref[(g * width + i) * width : (g * width + i + 1) * width, :]
            for g in range(groups)
        ]
        turned = jnp.concatenate(rows, axis=0).T
        thin_ref[0, pl.ds(i, taps, stride=width), :] = turned[:taps]
        turned = flat_ref[pl.ds(i, LANES, stride=width), :].T
        thin_ref[1, pl.ds(i, taps, stride=width), :] = turned[:taps]
    third = taps // 3 * LANES
    zero = jnp.zeros((third, LANES), BF)
    for n, dst in enumerate((f_ref, b_ref)):
        dst[0:third, LANES:] = zero
        dst[3 * third :, 0:LANES] = zero
        for t in range(taps):
            one = thin_ref[n, t * width : (t + 1) * width, :]
            full = jnp.where(keep, jnp.broadcast_to(one[None], keep.shape), 0.0)
            full = full.reshape(LANES, LANES).astype(BF)
            at = (t if n == 0 else taps - 1 - t) * LANES
            dst[at : at + LANES, 0:LANES] = full
            dst[third + at : third + at + LANES, LANES:] = full


def hidden_rows(x, lab, w, codes, wide, deep):
    pre = jnp.dot(x, w, preferred_element_type=F32)
    lab = lab.astype(F32)
    adds = []
    for y in range(wide):
        tag = jnp.broadcast_to(lab[:, y : y + 1], (deep, LANES))
        adds.append(jnp.where(tag < 0.5, codes[0], jnp.where(tag < 1.5, codes[1], codes[2])))
    return pre + jnp.concatenate(adds, axis=0)


def code_rows(code_ref, deep):
    return [jnp.broadcast_to(code_ref[i : i + 1, :], (deep, LANES)) for i in range(3)]


def own_kernel(
    micro, wide, deep, x_ref, ct_ref, lab_ref, w_ref, rw_ref, code_ref, *outs
):
    *kept, edge_ref = outs[3 * micro :]
    for src, dst in zip((x_ref, ct_ref, w_ref, rw_ref, code_ref), kept):
        dst[...] = src[...]
    c = lax.axis_index("chan")
    cells = wide * deep
    for m in range(micro):
        edge_ref[m * cells : (m + 1) * cells] = ct_ref[m, c]
    codes = code_rows(code_ref, deep)
    for m in range(micro):
        hs_ref, hid_ref, spre_ref = outs[3 * m : 3 * m + 3]
        for p in range(2):
            pre = hidden_rows(x_ref[m, p], lab_ref[m, p], w_ref[...], codes, wide, deep)
            q = gate(pre)
            h = pre * q
            hid_ref[p] = h.astype(BF)
            spre_ref[p] = slope(pre, q)
            store_shifts(hs_ref, p, h, wide, deep)


def forward_kernel(
    slot,
    wide,
    deep,
    own_ref,
    a_ref,
    b_ref,
    a2_ref,
    b2_ref,
    w_ref,
    code_ref,
    kf_ref,
    sconv_ref,
    mixed_ref,
    hs_ref,
):
    c = lax.axis_index("chan")
    cells = wide * deep
    codes = code_rows(code_ref, deep)
    start = slot * (cells + wide)
    for ref, plane in ((a_ref, 2 - c), (b_ref, 3 * c), (a2_ref, 1 + c), (b2_ref, 3 - 3 * c)):
        lab = ref[start + cells : start + cells + wide]
        pre = hidden_rows(ref[start : start + cells], lab, w_ref[...], codes, wide, deep)
        store_shifts(hs_ref, plane, pre * gate(pre), wide, deep)
    planes = [(hs_ref, 0), (hs_ref, 1), (own_ref, 0), (own_ref, 1), (hs_ref, 2), (hs_ref, 3)]
    for p, conv in enumerate(conv_pairs(planes, (1, 3), kf_ref, cells, deep)):
        q = gate(conv)
        sconv_ref[p] = slope(conv, q)
        if p in (1, 2):
            mixed_ref[p - 1] = (conv * q).astype(BF)


def backward_kernel(
    mode,
    m,
    sent_slot,
    wide,
    deep,
    taps,
    width,
    x_ref,
    ct_ref,
    cta_ref,
    cta2_ref,
    w_ref,
    rw_ref,
    kb_ref,
    spre_ref,
    sconv_ref,
    *rest,
):
    c = lax.axis_index("chan")
    cells = wide * deep
    tail = pl.ds(m * cells, cells)
    full = mode == "full"
    if mode == "first":
        base_ref, other_ref, gs_ref, br_ref = rest
        up_ref = ct_ref.at[m]
        halo, halo2 = cta_ref[tail], cta2_ref[tail]
    else:
        st_ref, st2_ref, dg_ref, dg2_ref, *rest = rest
        if full:
            hid_ref, mixed_ref, exp_in, red_in, kg_in, *rest = rest
            part_ref, up_ref, exp_ref, red_ref, kg_ref, gs_ref = rest
        else:
            base_ref, other_ref, gs_ref, br_ref, up_ref = rest
        here = pl.ds(sent_slot * cells, cells)
        last = lax.axis_index("section") == lax.axis_size("section") - 1

        @pl.when(last)
        def _():
            up_ref[0] = ct_ref[m, 0]
            up_ref[1] = ct_ref[m, 1]

        @pl.when(jnp.logical_not(last))
        def _():
            up_ref[c] = st_ref[here]
            up_ref[1 - c] = st2_ref[here]

        halo = jnp.where(last, cta_ref[tail], dg_ref[here])
        halo2 = jnp.where(last, cta2_ref[tail], dg2_ref[here])
    ups = ((up_ref[0], 1), (up_ref[1], 2), (halo, 3 - 3 * c), (halo2, 3 * c))
    for up, plane in ups:
        grad = nt_dot(up, rw_ref[...]) * sconv_ref[plane]
        store_shifts(gs_ref, plane, grad.astype(BF).astype(F32), wide, deep)
    if full:
        ups2 = up_ref[...].reshape(2 * cells, LANES)
        red = lax.dot_general(
            mixed_ref[...].reshape(2 * cells, LANES),
            ups2,
            (((0,), (0,)), ((), ())),
            preferred_element_type=F32,
        )
        red_ref[...] = red_in[...] + red
        groups = LANES // width
        keep = diagonal_mask(width)
        turned = [hid_ref[p].T for p in (0, 1)]
        left = jnp.concatenate(turned, axis=1)
        for dx in (-1, 0, 1):
            for dy in (-1, 0, 1):
                rows = slice((1 + dy) * deep, (1 + dy) * deep + cells)
                right = jnp.concatenate([gs_ref[1 + dx, rows, :], gs_ref[2 + dx, rows, :]], axis=0)
                dense = jnp.dot(left, right, preferred_element_type=F32)
                for j in range(3):
                    tap = 9 * (dx + 1) + 3 * (dy + 1) + j
                    block = dense[:, j * LANES : (j + 1) * LANES].reshape(groups, width, LANES)
                    thin = jnp.sum(jnp.where(keep, block, 0.0), axis=0)
                    at = slice((taps - 1 - tap) * width, (taps - tap) * width)
                    kg_ref[at] = kg_in[at] + thin
    planes = [(gs_ref, p) for p in range(4)]
    grads = []
    for p, grad_hidden in enumerate(conv_pairs(planes, (1,), kb_ref, cells, deep)):
        grad_pre = (grad_hidden * spre_ref[p]).astype(BF)
        branch = nt_dot(grad_pre, w_ref[...])
        if full:
            part_ref[p] = branch.astype(BF)
            grads.append(grad_pre)
        else:
            br_ref[p] = branch
    if full:
        exp_ref[...] = exp_in[...] + lax.dot_general(
            x_ref[m].reshape(2 * cells, LANES),
            jnp.concatenate(grads, axis=0),
            (((0,), (0,)), ((), ())),
            preferred_element_type=F32,
        )
    else:
        base_ref[...] = up_ref[c].astype(F32) + br_ref[c]
        other_ref[...] = br_ref[1 - c].astype(BF)


def emit_kernel(micro, *refs):
    ins, out_ref = refs[:-1], refs[-1]
    for m in range(micro):
        up, mine, other = ins[3 * m : 3 * m + 3]
        both = mine[...].astype(F32) + other[...].astype(F32)
        out_ref[m] = (up[...].astype(F32) + both).astype(BF)


def finish_kernel(count, scale, taps, width, *refs):
    ins, outs, thin_ref = refs[:count], refs[count:-1], refs[-1]
    total = ins[0][...].astype(F32)
    for ref in ins[1:]:
        total = total + ref[...].astype(F32)
    total = total * scale
    outs[0][...] = total[0:LANES]
    outs[1][...] = total[LANES : 2 * LANES]
    thin_ref[0 : taps * width] = total[2 * LANES :]
    for i in range(width):
        turned = thin_ref[pl.ds(i, LANES, stride=width), :].T
        outs[2][:, i] = turned[:, :taps].reshape(LANES // width, width, taps)


def SENDS(micro):
    return [[m] for m in range(micro)]


def sds(shape, dtype):
    return jax.ShapeDtypeStruct(shape, dtype)


def params(mebibytes):
    return pltpu.CompilerParams(vmem_limit_bytes=mebibytes * 2**20)


def call(kernel, name, out_shape, args, scratch=(), in_specs=None, room=16):
    vmem = pl.BlockSpec(memory_space=pltpu.VMEM)
    outs = [vmem] * len(out_shape)
    return pl.pallas_call(
        kernel,
        in_specs=[vmem] * len(args) if in_specs is None else in_specs,
        out_specs=outs,
        out_shape=out_shape,
        scratch_shapes=list(scratch),
        name=name,
        cost_estimate=pl.CostEstimate(flops=2 * 10**9, bytes_accessed=4 * 2**20, transcendentals=0),
        compiler_params=params(room),
    )(*args)


def on_device(
    section_inputs, cotangent, phase_labels, expand_weight, phase_code, kernel, reduce_weight
):
    _, micro, depth, wide, deep, trunk = section_inputs.shape
    cells = wide * deep
    taps, groups, width = kernel.shape[1], kernel.shape[2], kernel.shape[3]
    assert depth == 2 and lax.axis_size("chan") == 2
    assert trunk == LANES and groups * width == LANES
    spaces, sections = lax.axis_size("space"), lax.axis_size("section")
    scale = 1.0 / math.sqrt(micro * depth * spaces * cells)

    x = section_inputs[0].reshape(micro, depth, cells, trunk)
    ct = cotangent.reshape(micro, depth, cells, trunk)
    w, rw = expand_weight[0], reduce_weight[0]
    code = jnp.pad(phase_code[0], ((0, 8 - phase_code.shape[1]), (0, 0)))
    kern = kernel[0].transpose(1, 2, 3, 0)

    away = [(k, c, (k + 2 * c - 1) % spaces) for k in range(spaces) for c in (0, 1)]
    back = [(k, c, (k - 2 * c + 1) % spaces) for k in range(spaces) for c in (0, 1)]
    route_a = [(2 * k + c, 2 * t + c) for k, c, t in away]
    route_b = [(2 * k + c, 2 * t + c) for k, c, t in back]
    route_d = [
        ((k * sections + s) * 2 + c, (t * sections + (s - 1) % sections) * 2 + c)
        for k, c, t in away
        for s in range(sections)
    ]
    route_s = [(s, (s - 1) % sections) for s in range(sections)]

    def swap(v):
        return lax.ppermute(v, "chan", [(0, 1), (1, 0)])

    rows = cells + wide
    hbm = pl.BlockSpec(memory_space=pltpu.HBM)
    packed, lab = call(
        functools.partial(pack_kernel, micro, cells, wide),
        "pack",
        [sds((micro * rows, LANES), BF), sds((micro, depth, deep, LANES), BF)],
        (x, phase_labels),
        [
            pltpu.VMEM(phase_labels.shape, jnp.int32),
            pltpu.SemaphoreType.DMA((micro + 1,)),
        ],
        [hbm, hbm],
        60,
    )
    plane2, plane4, flat = (2, cells, LANES), (4, cells, LANES), (cells, LANES)
    pad_rows = cells + 2 * deep
    square, thin = (LANES, LANES), (taps * width, LANES)
    dense_f, dense_b = call(
        functools.partial(weights_kernel, taps, width),
        "weights",
        [sds((4 * taps // 3 * LANES, 2 * LANES), BF)] * 2,
        (kern,),
        [pltpu.VMEM((LANES * width, LANES), F32), pltpu.VMEM((2,) + thin, F32)],
    )
    *owned, x, ct, w, rw, code, edge = call(
        functools.partial(own_kernel, micro, wide, deep),
        "own",
        [sds((2, pad_rows, 3 * LANES), BF), sds(plane2, BF), sds(plane2, F32)] * micro
        + [sds(v.shape, v.dtype) for v in (x, ct, w, rw, code)]
        + [sds((micro * cells, LANES), BF)],
        (x, ct, lab, w, rw, code),
    )
    a = lax.ppermute(packed, ("space", "chan"), route_a)
    b = lax.ppermute(packed, ("space", "chan"), route_b)
    a, b, dense_f, dense_b, *owned = lax.optimization_barrier((a, b, dense_f, dense_b, *owned))
    halos = (a, b, swap(a), swap(b))
    edge = lax.ppermute(edge, ("space", "chan"), route_a)

    def joined(pairs):
        outs = [(base + swap(other).astype(F32)).astype(BF) for base, other in pairs]
        return outs[0] if len(outs) == 1 else jnp.concatenate(outs, axis=0)

    def send_on(out):
        st = lax.ppermute(out, "section", route_s)
        dg = lax.ppermute(out, ("space", "section", "chan"), route_d)
        return st, dg

    def after(arrays, first):
        *arrays, _ = lax.optimization_barrier((*arrays, first))
        return arrays

    def shared(st, dg):
        return st, swap(st), dg, swap(dg)

    def back_pass(mode, m, extra, extra_out=()):
        outs = [sds(flat, F32), sds(flat, BF)] if mode != "full" else [sds(plane2, BF)] * 2
        scratch = [pltpu.VMEM((4, pad_rows, 3 * LANES), BF)]
        if mode != "full":
            scratch.append(pltpu.VMEM(plane2, F32))
        if mode == "light":
            scratch.append(pltpu.VMEM(plane2, BF))
        return call(
            functools.partial(backward_kernel, mode, m, sent_slot[m], wide, deep, taps, width),
            "backward_" + mode,
            outs + list(extra_out),
            (x, ct, *edges, w, rw, dense_b, spre[m], sconv[m], *extra),
            scratch,
        )

    sconv, mixed, sent = [], [], []
    sends = SENDS(micro)
    sender = [n for n, group in enumerate(sends) for _ in group]
    sent_slot = [i for group in sends for i in range(len(group))]
    spre = [owned[3 * m + 2] for m in range(micro)]
    for m in range(micro):
        if m:
            (code,) = after((code,), sconv[-1])
        con, mix = call(
            functools.partial(forward_kernel, m, wide, deep),
            "forward",
            [sds(plane4, F32), sds(plane2, BF)],
            (owned[3 * m], *halos, w, code, dense_f),
            [pltpu.VMEM((4, pad_rows, 3 * LANES), BF)],
        )
        sconv.append(con)
        mixed.append(mix)
    (edge,) = after((edge,), sconv[-1])
    edges = (edge, swap(edge))
    pending = []
    for m in range(micro):
        if m == 0:
            (sconv[m],) = after((sconv[m],), sconv[-1])
        if pending and len(pending) == len(sends[len(sent)]):
            out, sconv[m] = lax.optimization_barrier((joined(pending), sconv[m]))
            sent.append(send_on(out))
            pending = []
        pending.append(back_pass("first", m, ()))
    out = joined(pending)
    sent = [after(pair, pending[-1][1]) for pair in sent[:1]] + [after(pair, pending[-1][1]) for pair in sent[1:]]
    sent.append(send_on(out))
    ups = [shared(*pair) for pair in sent]

    rank = lax.axis_index("section")
    for stage in range(1, sections - 1):
        fresh = []
        for group in sends:
            out = joined([back_pass("light", m, ups[sender[m]]) for m in group])
            fresh.append(shared(*send_on(out)))
        mine = rank == sections - 2 - stage
        ups = [
            tuple(jnp.where(mine, n, o) for n, o in zip(new, old)) for new, old in zip(fresh, ups)
        ]
    sum_shapes = [sds(s, F32) for s in (square, square, thin)]
    sums = [jnp.zeros(s.shape, F32) for s in sum_shapes]
    pieces = []
    for m in range(micro):
        extra = (*ups[sender[m]], owned[3 * m + 1], mixed[m], *sums)
        part, up, *sums = back_pass("full", m, extra, sum_shapes)
        if m == 0 and sections == 2 and sender[-1] > 0:
            ups[-1] = shared(*after(sent[-1], part))
        pieces += [up, part, swap(part)]

    grads = jnp.concatenate([s.astype(BF) for s in sums], axis=0)
    if spaces == 4:
        near = [(k, k ^ 1) for k in range(spaces)]
        far = [(k, k ^ 3) for k in range(spaces)]
        grads = grads + lax.ppermute(grads, "space", near)
        copies = [grads, lax.ppermute(grads, "space", far)]
    else:
        copies = [lax.psum(grads, "space")]
    (out,) = call(
        functools.partial(emit_kernel, micro), "emit", [sds((micro,) + plane2, BF)], pieces
    )
    *copies, out = lax.optimization_barrier((*copies, out))
    exp_g, red_g, kg = call(
        functools.partial(finish_kernel, len(copies), scale, taps, width),
        "finish",
        [sds(square, F32), sds(square, F32), sds((groups, width, width, taps), F32)],
        copies,
        [pltpu.VMEM((LANES * width, LANES), F32)],
    )
    kg = kg.transpose(3, 0, 1, 2)
    return (
        out.reshape(section_inputs.shape),
        exp_g[None],
        kg[None],
        red_g[None],
    )


def solution(mesh):
    placed = (
        P("section", "parts", "space", None, None, None),
        P("parts", "space", None, None, None),
        P("parts", "space", None, None),
        P("section", None, "chan"),
        P("section", None, "chan"),
        P("section", None, "chan", None, None),
        P("section", "chan", None),
    )
    return jax.shard_map(
        on_device,
        mesh=mesh,
        in_specs=placed,
        out_specs=(
            P("section", "parts", "space", None, None, None),
            P(("parts", "section"), None, "chan"),
            P(("parts", "section"), None, "chan", None, None),
            P(("parts", "section"), "chan", None),
        ),
        check_vma=False,
    )
```

```python
import functools
import math

import jax
import jax.numpy as jnp
from jax import lax
from jax.experimental import pallas as pl
from jax.experimental.pallas import tpu as pltpu
from jax.sharding import PartitionSpec as P

BF = jnp.bfloat16
F32 = jnp.float32
LANES = 128


def gate(v):
    return 0.5 + 0.5 * jnp.tanh(0.5 * v)


def slope(v, q):
    return q * (1.0 + v * (1.0 - q))


def nt_dot(a, b):
    return lax.dot_general(a, b, (((1,), (1,)), ((), ())), preferred_element_type=F32)


def store_shifts(ref, plane, value, wide, deep):
    cells = wide * deep
    cube = value.reshape(wide, deep, LANES)
    for j, turn in enumerate((1, 0, deep - 1)):
        moved = cube if turn == 0 else pltpu.roll(cube, turn, axis=1)
        flat = moved.reshape(cells, LANES).astype(BF)
        lanes = slice(j * LANES, (j + 1) * LANES)
        ref[plane, deep : deep + cells, lanes] = flat
        ref[plane, 0:deep, lanes] = flat[cells - deep :]
        ref[plane, deep + cells : cells + 2 * deep, lanes] = flat[:deep]


def pair_rows(planes, first, cells, deep):
    parts = []
    for at in range(first - 1, first + 3):
        ref, plane = planes[at]
        for dy in range(3):
            parts.append(ref[plane, dy * deep : dy * deep + cells, :])
    return jnp.concatenate(parts, axis=1)


def conv_pairs(planes, firsts, weights, cells, deep):
    rows = [pair_rows(planes, first, cells, deep) for first in firsts]
    rows = rows[0] if len(rows) == 1 else jnp.concatenate(rows, axis=0)
    both = jnp.dot(rows, weights[...], preferred_element_type=F32)
    outs = []
    for n in range(len(firsts)):
        for o in range(2):
            outs.append(both[n * cells : (n + 1) * cells, o * LANES : (o + 1) * LANES])
    return outs


def pack_kernel(
    micro, cells, wide, x_ref, ct_ref, tag_ref, a_ref, b_ref, own_ref, lab_ref, sem
):
    tags = pltpu.make_async_copy(tag_ref, lab_ref, sem.at[2 * micro + 1])
    tags.start()
    c = lax.axis_index("chan")
    copies = []
    for m in range(micro):
        for n, out_ref in enumerate((a_ref, b_ref)):
            spot = out_ref.at[pl.ds(m * (cells + wide), cells)]
            copy = pltpu.make_async_copy(x_ref.at[m, c], spot, sem.at[2 * m + n])
            copy.start()
            copies.append(copy)
    spot = a_ref.at[pl.ds(micro * (cells + wide), cells)]
    copy = pltpu.make_async_copy(ct_ref.at[0, c], spot, sem.at[2 * micro])
    copy.start()
    copies.append(copy)
    deep = lab_ref.shape[3]
    tags.wait()
    row = lax.broadcasted_iota(jnp.int32, (LANES, LANES), 0)
    lane = lax.broadcasted_iota(jnp.int32, (LANES, LANES), 1)
    eye = jnp.where(row == lane, 1.0, 0.0)[:deep, :deep].astype(BF)
    for m in range(micro):
        for p in range(2):
            own_ref[m, p] = jnp.zeros((deep, LANES), BF)
            turned = nt_dot(eye, lab_ref[m, p].astype(F32).astype(BF))
            own_ref[m, p, :, 0:wide] = turned.astype(BF)
        for out_ref in (a_ref, b_ref):
            out_ref[m * (cells + wide) + cells : (m + 1) * (cells + wide)] = own_ref[m, c]
    for copy in copies:
        copy.wait()


def diagonal_mask(width):
    groups = LANES // width
    g = lax.broadcasted_iota(jnp.int32, (groups, width, LANES), 0)
    lane = lax.broadcasted_iota(jnp.int32, (groups, width, LANES), 2)
    return g == lane // width


def weights_kernel(taps, width, k_ref, f_ref, b_ref, flat_ref, thin_ref):
    groups = LANES // width
    keep = diagonal_mask(width)
    flat_ref[:, 0:taps] = k_ref[...].astype(F32).reshape(groups * width * width, taps)
    for i in range(width):
        rows = [
            flat_ref[(g * width + i) * width : (g * width + i + 1) * width, :]
            for g in range(groups)
        ]
        turned = jnp.concatenate(rows, axis=0).T
        thin_ref[0, pl.ds(i, taps, stride=width), :] = turned[:taps]
        turned = flat_ref[pl.ds(i, LANES, stride=width), :].T
        thin_ref[1, pl.ds(i, taps, stride=width), :] = turned[:taps]
    third = taps // 3 * LANES
    zero = jnp.zeros((third, LANES), BF)
    for n, dst in enumerate((f_ref, b_ref)):
        dst[0:third, LANES:] = zero
        dst[3 * third :, 0:LANES] = zero
        for t in range(taps):
            one = thin_ref[n, t * width : (t + 1) * width, :]
            full = jnp.where(keep, jnp.broadcast_to(one[None], keep.shape), 0.0)
            full = full.reshape(LANES, LANES).astype(BF)
            at = (t if n == 0 else taps - 1 - t) * LANES
            dst[at : at + LANES, 0:LANES] = full
            dst[third + at : third + at + LANES, LANES:] = full


def hidden_rows(x, lab, w, codes, wide, deep):
    pre = jnp.dot(x, w, preferred_element_type=F32)
    lab = lab.astype(F32)
    adds = []
    for y in range(wide):
        tag = jnp.broadcast_to(lab[:, y : y + 1], (deep, LANES))
        adds.append(jnp.where(tag < 0.5, codes[0], jnp.where(tag < 1.5, codes[1], codes[2])))
    return pre + jnp.concatenate(adds, axis=0)


def code_rows(code_ref, deep):
    return [jnp.broadcast_to(code_ref[i : i + 1, :], (deep, LANES)) for i in range(3)]


def own_kernel(
    micro, wide, deep, x_ref, ct_ref, lab_ref, w_ref, rw_ref, code_ref, *outs
):
    *kept, edge_ref = outs[3 * micro :]
    for src, dst in zip((x_ref, ct_ref, w_ref, rw_ref, code_ref), kept):
        dst[...] = src[...]
    c = lax.axis_index("chan")
    cells = wide * deep
    for m in range(1, micro):
        edge_ref[(m - 1) * cells : m * cells] = ct_ref[m, c]
    codes = code_rows(code_ref, deep)
    for m in range(micro):
        hs_ref, hid_ref, spre_ref = outs[3 * m : 3 * m + 3]
        for p in range(2):
            pre = hidden_rows(x_ref[m, p], lab_ref[m, p], w_ref[...], codes, wide, deep)
            q = gate(pre)
            h = pre * q
            hid_ref[p] = h.astype(BF)
            spre_ref[p] = slope(pre, q)
            store_shifts(hs_ref, p, h, wide, deep)


def forward_kernel(
    slot,
    wide,
    deep,
    own_ref,
    a_ref,
    b_ref,
    a2_ref,
    b2_ref,
    w_ref,
    code_ref,
    kf_ref,
    sconv_ref,
    mixed_ref,
    hs_ref,
):
    c = lax.axis_index("chan")
    cells = wide * deep
    codes = code_rows(code_ref, deep)
    start = slot * (cells + wide)
    first = c == 0
    sources = ((b_ref, b2_ref), (a2_ref, a_ref), (a_ref, a2_ref), (b2_ref, b_ref))
    for plane, (yes, no) in enumerate(sources):
        rows = slice(start, start + cells + wide)
        both = jnp.where(first, yes[rows], no[rows])
        pre = hidden_rows(both[:cells], both[cells:], w_ref[...], codes, wide, deep)
        store_shifts(hs_ref, plane, pre * gate(pre), wide, deep)
    planes = [(hs_ref, 0), (hs_ref, 1), (own_ref, 0), (own_ref, 1), (hs_ref, 2), (hs_ref, 3)]
    for p, conv in enumerate(conv_pairs(planes, (1, 3), kf_ref, cells, deep)):
        q = gate(conv)
        sconv_ref[p] = slope(conv, q)
        if p in (1, 2):
            mixed_ref[p - 1] = (conv * q).astype(BF)


def backward_kernel(
    mode,
    m,
    sent_slot,
    tail_start,
    wide,
    deep,
    taps,
    width,
    x_ref,
    ct_ref,
    cta_ref,
    cta2_ref,
    w_ref,
    rw_ref,
    kb_ref,
    spre_ref,
    sconv_ref,
    *rest,
):
    c = lax.axis_index("chan")
    cells = wide * deep
    tail = pl.ds(tail_start, cells)
    full = mode == "full"
    if mode == "first":
        base_ref, other_ref, gs_ref, br_ref = rest
        up_ref = ct_ref.at[m]
        halo, halo2 = cta_ref[tail], cta2_ref[tail]
        own = (ct_ref[m, 0], ct_ref[m, 1])
    else:
        st_ref, st2_ref, dg_ref, dg2_ref, *rest = rest
        if full:
            hid_ref, mixed_ref, exp_in, red_in, kg_in, *rest = rest
            part_ref, up_ref, exp_ref, red_ref, kg_ref, gs_ref = rest
        else:
            base_ref, other_ref, gs_ref, br_ref, up_ref = rest
        here = pl.ds(sent_slot * cells, cells)
        last = lax.axis_index("section") == lax.axis_size("section") - 1

        mine, theirs = st_ref[here], st2_ref[here]
        own = (
            jnp.where(last, ct_ref[m, 0], jnp.where(c == 0, mine, theirs)),
            jnp.where(last, ct_ref[m, 1], jnp.where(c == 0, theirs, mine)),
        )
        for p in (0, 1):
            up_ref[p] = own[p]
        halo = jnp.where(last, cta_ref[tail], dg_ref[here])
        halo2 = jnp.where(last, cta2_ref[tail], dg2_ref[here])
    below = jnp.where(c == 0, halo2, halo)
    above = jnp.where(c == 0, halo, halo2)
    for plane, up in enumerate((below, *own, above)):
        grad = nt_dot(up, rw_ref[...]) * sconv_ref[plane]
        store_shifts(gs_ref, plane, grad.astype(BF).astype(F32), wide, deep)
    if full:
        ups2 = up_ref[...].reshape(2 * cells, LANES)
        red = lax.dot_general(
            mixed_ref[...].reshape(2 * cells, LANES),
            ups2,
            (((0,), (0,)), ((), ())),
            preferred_element_type=F32,
        )
        red_ref[...] = red_in[...] + red
        groups = LANES // width
        keep = diagonal_mask(width)
        turned = [hid_ref[p].T for p in (0, 1)]
        left = jnp.concatenate(turned, axis=1)
        for dx in (-1, 0, 1):
            for dy in (-1, 0, 1):
                rows = slice((1 + dy) * deep, (1 + dy) * deep + cells)
                right = jnp.concatenate([gs_ref[1 + dx, rows, :], gs_ref[2 + dx, rows, :]], axis=0)
                dense = jnp.dot(left, right, preferred_element_type=F32)
                for j in range(3):
                    tap = 9 * (dx + 1) + 3 * (dy + 1) + j
                    block = dense[:, j * LANES : (j + 1) * LANES].reshape(groups, width, LANES)
                    thin = jnp.sum(jnp.where(keep, block, 0.0), axis=0)
                    at = slice((taps - 1 - tap) * width, (taps - tap) * width)
                    kg_ref[at] = kg_in[at] + thin
    planes = [(gs_ref, p) for p in range(4)]
    grads = []
    for p, grad_hidden in enumerate(conv_pairs(planes, (1,), kb_ref, cells, deep)):
        grad_pre = (grad_hidden * spre_ref[p]).astype(BF)
        branch = nt_dot(grad_pre, w_ref[...])
        if full:
            part_ref[p] = branch.astype(BF)
            grads.append(grad_pre)
        else:
            br_ref[p] = branch
    if full:
        exp_ref[...] = exp_in[...] + lax.dot_general(
            x_ref[m].reshape(2 * cells, LANES),
            jnp.concatenate(grads, axis=0),
            (((0,), (0,)), ((), ())),
            preferred_element_type=F32,
        )
    else:
        base_ref[...] = up_ref[c].astype(F32) + br_ref[c]
        other_ref[...] = br_ref[1 - c].astype(BF)


def emit_kernel(micro, *refs):
    ins, out_ref = refs[:-1], refs[-1]
    for m in range(micro):
        up, mine, other = ins[3 * m : 3 * m + 3]
        both = mine[...].astype(F32) + other[...].astype(F32)
        out_ref[m] = (up[...].astype(F32) + both).astype(BF)


def finish_kernel(count, scale, taps, width, *refs):
    ins, outs, thin_ref = refs[:count], refs[count:-1], refs[-1]
    total = ins[0][...].astype(F32)
    for ref in ins[1:]:
        total = total + ref[...].astype(F32)
    total = total * scale
    outs[0][...] = total[0:LANES]
    outs[1][...] = total[LANES : 2 * LANES]
    thin_ref[0 : taps * width] = total[2 * LANES :]
    for i in range(width):
        turned = thin_ref[pl.ds(i, LANES, stride=width), :].T
        outs[2][:, i] = turned[:, :taps].reshape(LANES // width, width, taps)


def SENDS(micro):
    return [[m] for m in range(micro)]


def sds(shape, dtype):
    return jax.ShapeDtypeStruct(shape, dtype)


def params(mebibytes):
    return pltpu.CompilerParams(vmem_limit_bytes=mebibytes * 2**20)


def call(kernel, name, out_shape, args, scratch=(), in_specs=None, room=16):
    vmem = pl.BlockSpec(memory_space=pltpu.VMEM)
    outs = [vmem] * len(out_shape)
    return pl.pallas_call(
        kernel,
        in_specs=[vmem] * len(args) if in_specs is None else in_specs,
        out_specs=outs,
        out_shape=out_shape,
        scratch_shapes=list(scratch),
        name=name,
        cost_estimate=pl.CostEstimate(flops=2 * 10**9, bytes_accessed=4 * 2**20, transcendentals=0),
        compiler_params=params(room),
    )(*args)


def on_device(
    section_inputs, cotangent, phase_labels, expand_weight, phase_code, kernel, reduce_weight
):
    _, micro, depth, wide, deep, trunk = section_inputs.shape
    cells = wide * deep
    taps, groups, width = kernel.shape[1], kernel.shape[2], kernel.shape[3]
    assert depth == 2 and lax.axis_size("chan") == 2
    assert trunk == LANES and groups * width == LANES
    spaces, sections = lax.axis_size("space"), lax.axis_size("section")
    scale = 1.0 / math.sqrt(micro * depth * spaces * cells)

    x = section_inputs[0].reshape(micro, depth, cells, trunk)
    ct = cotangent.reshape(micro, depth, cells, trunk)
    w, rw = expand_weight[0], reduce_weight[0]
    code = jnp.pad(phase_code[0], ((0, 8 - phase_code.shape[1]), (0, 0)))
    kern = kernel[0].transpose(1, 2, 3, 0)

    away = [(k, c, (k + 2 * c - 1) % spaces) for k in range(spaces) for c in (0, 1)]
    back = [(k, c, (k - 2 * c + 1) % spaces) for k in range(spaces) for c in (0, 1)]
    route_a = [(2 * k + c, 2 * t + c) for k, c, t in away]
    route_b = [(2 * k + c, 2 * t + c) for k, c, t in back]
    route_d = [
        ((k * sections + s) * 2 + c, (t * sections + (s - 1) % sections) * 2 + c)
        for k, c, t in away
        for s in range(sections)
    ]
    route_s = [(s, (s - 1) % sections) for s in range(sections)]

    def swap(v):
        return lax.ppermute(v, "chan", [(0, 1), (1, 0)])

    rows = cells + wide
    hbm = pl.BlockSpec(memory_space=pltpu.HBM)
    packed_a, packed_b, lab = call(
        functools.partial(pack_kernel, micro, cells, wide),
        "pack",
        [
            sds((micro * rows + cells, LANES), BF),
            sds((micro * rows, LANES), BF),
            sds((micro, depth, deep, LANES), BF),
        ],
        (x, ct, phase_labels),
        [
            pltpu.VMEM(phase_labels.shape, jnp.int32),
            pltpu.SemaphoreType.DMA((2 * micro + 2,)),
        ],
        [hbm, hbm, hbm],
        60,
    )
    plane2, plane4, flat = (2, cells, LANES), (4, cells, LANES), (cells, LANES)
    pad_rows = cells + 2 * deep
    square, thin = (LANES, LANES), (taps * width, LANES)
    dense_f, dense_b = call(
        functools.partial(weights_kernel, taps, width),
        "weights",
        [sds((4 * taps // 3 * LANES, 2 * LANES), BF)] * 2,
        (kern,),
        [pltpu.VMEM((LANES * width, LANES), F32), pltpu.VMEM((2,) + thin, F32)],
    )
    *owned, x, ct, w, rw, code, edge = call(
        functools.partial(own_kernel, micro, wide, deep),
        "own",
        [sds((2, pad_rows, 3 * LANES), BF), sds(plane2, BF), sds(plane2, F32)] * micro
        + [sds(v.shape, v.dtype) for v in (x, ct, w, rw, code)]
        + [sds((max(1, micro - 1) * cells, LANES), BF)],
        (x, ct, lab, w, rw, code),
    )
    a = lax.ppermute(packed_a, ("space", "chan"), route_a)
    b = lax.ppermute(packed_b, ("space", "chan"), route_b)
    a, b, dense_f, dense_b, *owned = lax.optimization_barrier((a, b, dense_f, dense_b, *owned))
    halos = (a, b, swap(a), swap(b))
    edge = lax.ppermute(edge, ("space", "chan"), route_a)

    def joined(pairs):
        outs = [(base + swap(other).astype(F32)).astype(BF) for base, other in pairs]
        return outs[0] if len(outs) == 1 else jnp.concatenate(outs, axis=0)

    def send_on(out):
        st = lax.ppermute(out, "section", route_s)
        dg = lax.ppermute(out, ("space", "section", "chan"), route_d)
        return st, dg

    def after(arrays, first):
        *arrays, _ = lax.optimization_barrier((*arrays, first))
        return arrays

    def shared(st, dg):
        return st, swap(st), dg, swap(dg)

    def back_pass(mode, m, extra, extra_out=()):
        outs = [sds(flat, F32), sds(flat, BF)] if mode != "full" else [sds(plane2, BF)] * 2
        scratch = [pltpu.VMEM((4, pad_rows, 3 * LANES), BF)]
        if mode != "full":
            scratch.append(pltpu.VMEM(plane2, F32))
        if mode == "light":
            scratch.append(pltpu.VMEM(plane2, BF))
        return call(
            functools.partial(backward_kernel, mode, m, sent_slot[m], tails[m], wide, deep, taps, width),
            "backward_" + mode,
            outs + list(extra_out),
            (x, ct, *edges[m], w, rw, dense_b, spre[m], sconv[m], *extra),
            scratch,
        )

    sconv, mixed, sent = [], [], []
    sends = SENDS(micro)
    sender = [n for n, group in enumerate(sends) for _ in group]
    sent_slot = [i for group in sends for i in range(len(group))]
    spre = [owned[3 * m + 2] for m in range(micro)]
    tails = [micro * rows] + [m * cells for m in range(micro - 1)]
    edges = [(halos[0], halos[2])]
    pending, previous = [], None
    for m in range(micro):
        con, mix = call(
            functools.partial(forward_kernel, m, wide, deep),
            "forward",
            [sds(plane4, F32), sds(plane2, BF)],
            (owned[3 * m], *halos, w, code, dense_f),
            [pltpu.VMEM((4, pad_rows, 3 * LANES), BF)],
        )
        sconv.append(con)
        mixed.append(mix)
        (code,) = after((code,), con)
        if m == 0:
            previous = back_pass("first", 0, ())
            (code,) = after((code,), previous[1])
            sent.append(send_on(joined([previous])))
    (edge,) = after((edge,), sconv[-1])
    edges += [(edge, swap(edge))] * (micro - 1)
    for m in range(1, micro):
        (sconv[m],) = after((sconv[m],), previous[1])
        previous = back_pass("first", m, ())
        sent.append(send_on(joined([previous])))
    sent[0] = after(sent[0], previous[1])
    ups = [shared(*pair) for pair in sent]

    rank = lax.axis_index("section")
    for stage in range(1, sections - 1):
        fresh = []
        for group in sends:
            out = joined([back_pass("light", m, ups[sender[m]]) for m in group])
            fresh.append(shared(*send_on(out)))
        mine = rank == sections - 2 - stage
        ups = [
            tuple(jnp.where(mine, n, o) for n, o in zip(new, old)) for new, old in zip(fresh, ups)
        ]
    sum_shapes = [sds(s, F32) for s in (square, square, thin)]
    sums = [jnp.zeros(s.shape, F32) for s in sum_shapes]
    pieces = []
    for m in range(micro):
        extra = (*ups[sender[m]], owned[3 * m + 1], mixed[m], *sums)
        part, up, *sums = back_pass("full", m, extra, sum_shapes)
        if m == 0 and sections == 2 and sender[-1] > 0:
            ups[-1] = shared(*after(sent[-1], part))
        pieces += [up, part, swap(part)]

    grads = jnp.concatenate([s.astype(BF) for s in sums], axis=0)
    if spaces == 4:
        near = [(k, k ^ 1) for k in range(spaces)]
        far = [(k, k ^ 3) for k in range(spaces)]
        grads = grads + lax.ppermute(grads, "space", near)
        copies = [grads, lax.ppermute(grads, "space", far)]
    else:
        copies = [lax.psum(grads, "space")]
    (out,) = call(
        functools.partial(emit_kernel, micro), "emit", [sds((micro,) + plane2, BF)], pieces
    )
    *copies, out = lax.optimization_barrier((*copies, out))
    exp_g, red_g, kg = call(
        functools.partial(finish_kernel, len(copies), scale, taps, width),
        "finish",
        [sds(square, F32), sds(square, F32), sds((groups, width, width, taps), F32)],
        copies,
        [pltpu.VMEM((LANES * width, LANES), F32)],
    )
    kg = kg.transpose(3, 0, 1, 2)
    return (
        out.reshape(section_inputs.shape),
        exp_g[None],
        kg[None],
        red_g[None],
    )


def solution(mesh):
    placed = (
        P("section", "parts", "space", None, None, None),
        P("parts", "space", None, None, None),
        P("parts", "space", None, None),
        P("section", None, "chan"),
        P("section", None, "chan"),
        P("section", None, "chan", None, None),
        P("section", "chan", None),
    )
    return jax.shard_map(
        on_device,
        mesh=mesh,
        in_specs=placed,
        out_specs=(
            P("section", "parts", "space", None, None, None),
            P(("parts", "section"), None, "chan"),
            P(("parts", "section"), None, "chan", None, None),
            P(("parts", "section"), "chan", None),
        ),
        check_vma=False,
    )
```

```python
import functools
import math

import jax
import jax.numpy as jnp
from jax import lax
from jax.experimental import pallas as pl
from jax.experimental.pallas import tpu as pltpu
from jax.sharding import PartitionSpec as P

BF = jnp.bfloat16
F32 = jnp.float32
LANES = 128


def gate(v):
    return 0.5 + 0.5 * jnp.tanh(0.5 * v)


def slope(v, q):
    return q * (1.0 + v * (1.0 - q))


def nt_dot(a, b):
    return lax.dot_general(a, b, (((1,), (1,)), ((), ())), preferred_element_type=F32)


def store_shifts(ref, plane, value, wide, deep):
    cells = wide * deep
    cube = value.reshape(wide, deep, LANES)
    for j, turn in enumerate((1, 0, deep - 1)):
        moved = cube if turn == 0 else pltpu.roll(cube, turn, axis=1)
        flat = moved.reshape(cells, LANES).astype(BF)
        lanes = slice(j * LANES, (j + 1) * LANES)
        ref[plane, deep : deep + cells, lanes] = flat
        ref[plane, 0:deep, lanes] = flat[cells - deep :]
        ref[plane, deep + cells : cells + 2 * deep, lanes] = flat[:deep]


def pair_rows(planes, first, cells, deep):
    parts = []
    for at in range(first - 1, first + 3):
        ref, plane = planes[at]
        for dy in range(3):
            parts.append(ref[plane, dy * deep : dy * deep + cells, :])
    return jnp.concatenate(parts, axis=1)


def conv_pairs(planes, firsts, weights, cells, deep):
    rows = [pair_rows(planes, first, cells, deep) for first in firsts]
    rows = rows[0] if len(rows) == 1 else jnp.concatenate(rows, axis=0)
    both = jnp.dot(rows, weights[...], preferred_element_type=F32)
    outs = []
    for n in range(len(firsts)):
        for o in range(2):
            outs.append(both[n * cells : (n + 1) * cells, o * LANES : (o + 1) * LANES])
    return outs


def pack_kernel(
    micro, cells, wide, x_ref, ct_ref, tag_ref, a_ref, b_ref, own_ref, lab_ref, sem
):
    tags = pltpu.make_async_copy(tag_ref, lab_ref, sem.at[2 * micro + 1])
    tags.start()
    c = lax.axis_index("chan")
    copies = []
    for m in range(micro):
        for n, out_ref in enumerate((a_ref, b_ref)):
            spot = out_ref.at[pl.ds(m * (cells + wide), cells)]
            copy = pltpu.make_async_copy(x_ref.at[m, c], spot, sem.at[2 * m + n])
            copy.start()
            copies.append(copy)
    spot = a_ref.at[pl.ds(micro * (cells + wide), cells)]
    copy = pltpu.make_async_copy(ct_ref.at[0, c], spot, sem.at[2 * micro])
    copy.start()
    copies.append(copy)
    deep = lab_ref.shape[3]
    tags.wait()
    row = lax.broadcasted_iota(jnp.int32, (LANES, LANES), 0)
    lane = lax.broadcasted_iota(jnp.int32, (LANES, LANES), 1)
    eye = jnp.where(row == lane, 1.0, 0.0)[:deep, :deep].astype(BF)
    for m in range(micro):
        for p in range(2):
            own_ref[m, p] = jnp.zeros((deep, LANES), BF)
            turned = nt_dot(eye, lab_ref[m, p].astype(F32).astype(BF))
            own_ref[m, p, :, 0:wide] = turned.astype(BF)
        for out_ref in (a_ref, b_ref):
            out_ref[m * (cells + wide) + cells : (m + 1) * (cells + wide)] = own_ref[m, c]
    for copy in copies:
        copy.wait()


def diagonal_mask(width):
    groups = LANES // width
    g = lax.broadcasted_iota(jnp.int32, (groups, width, LANES), 0)
    lane = lax.broadcasted_iota(jnp.int32, (groups, width, LANES), 2)
    return g == lane // width


def weights_kernel(taps, width, k_ref, f_ref, b_ref, flat_ref, thin_ref):
    groups = LANES // width
    keep = diagonal_mask(width)
    flat_ref[:, 0:taps] = k_ref[...].astype(F32).reshape(groups * width * width, taps)
    for i in range(width):
        rows = [
            flat_ref[(g * width + i) * width : (g * width + i + 1) * width, :]
            for g in range(groups)
        ]
        turned = jnp.concatenate(rows, axis=0).T
        thin_ref[0, pl.ds(i, taps, stride=width), :] = turned[:taps]
        turned = flat_ref[pl.ds(i, LANES, stride=width), :].T
        thin_ref[1, pl.ds(i, taps, stride=width), :] = turned[:taps]
    third = taps // 3 * LANES
    zero = jnp.zeros((third, LANES), BF)
    for n, dst in enumerate((f_ref, b_ref)):
        dst[0:third, LANES:] = zero
        dst[3 * third :, 0:LANES] = zero
        for t in range(taps):
            one = thin_ref[n, t * width : (t + 1) * width, :]
            full = jnp.where(keep, jnp.broadcast_to(one[None], keep.shape), 0.0)
            full = full.reshape(LANES, LANES).astype(BF)
            at = (t if n == 0 else taps - 1 - t) * LANES
            dst[at : at + LANES, 0:LANES] = full
            dst[third + at : third + at + LANES, LANES:] = full


def hidden_rows(x, lab, w, codes, wide, deep):
    pre = jnp.dot(x, w, preferred_element_type=F32)
    lab = lab.astype(F32)
    adds = []
    for y in range(wide):
        tag = jnp.broadcast_to(lab[:, y : y + 1], (deep, LANES))
        adds.append(jnp.where(tag < 0.5, codes[0], jnp.where(tag < 1.5, codes[1], codes[2])))
    return pre + jnp.concatenate(adds, axis=0)


def code_rows(code_ref, deep):
    return [jnp.broadcast_to(code_ref[i : i + 1, :], (deep, LANES)) for i in range(3)]


def own_kernel(
    micro, wide, deep, x_ref, ct_ref, lab_ref, w_ref, rw_ref, code_ref, *outs
):
    *kept, edge_ref, flip_ref = outs[3 * micro :]
    for src, dst in zip((x_ref, ct_ref, w_ref, rw_ref, code_ref), kept):
        dst[...] = src[...]
    c = lax.axis_index("chan")
    cells = wide * deep
    for m in range(1, micro):
        edge_ref[(m - 1) * cells : m * cells] = ct_ref[m, c]
    codes = code_rows(code_ref, deep)
    for m in range(micro):
        hs_ref, hid_ref, spre_ref = outs[3 * m : 3 * m + 3]
        flip_ref[m] = x_ref[m].reshape(2 * cells, LANES).T
        for p in range(2):
            pre = hidden_rows(x_ref[m, p], lab_ref[m, p], w_ref[...], codes, wide, deep)
            q = gate(pre)
            h = pre * q
            hid_ref[:, p * cells : (p + 1) * cells] = h.astype(BF).T
            spre_ref[p] = slope(pre, q)
            store_shifts(hs_ref, p, h, wide, deep)


def forward_kernel(
    slot,
    wide,
    deep,
    own_ref,
    a_ref,
    b_ref,
    a2_ref,
    b2_ref,
    w_ref,
    code_ref,
    kf_ref,
    sconv_ref,
    mixed_ref,
    hs_ref,
):
    c = lax.axis_index("chan")
    cells = wide * deep
    codes = code_rows(code_ref, deep)
    start = slot * (cells + wide)
    first = c == 0
    sources = ((b_ref, b2_ref), (a2_ref, a_ref), (a_ref, a2_ref), (b2_ref, b_ref))
    for plane, (yes, no) in enumerate(sources):
        rows = slice(start, start + cells + wide)
        both = jnp.where(first, yes[rows], no[rows])
        pre = hidden_rows(both[:cells], both[cells:], w_ref[...], codes, wide, deep)
        store_shifts(hs_ref, plane, pre * gate(pre), wide, deep)
    planes = [(hs_ref, 0), (hs_ref, 1), (own_ref, 0), (own_ref, 1), (hs_ref, 2), (hs_ref, 3)]
    for p, conv in enumerate(conv_pairs(planes, (1, 3), kf_ref, cells, deep)):
        q = gate(conv)
        sconv_ref[p] = slope(conv, q)
        if p in (1, 2):
            mixed_ref[:, (p - 1) * cells : p * cells] = (conv * q).astype(BF).T


def backward_kernel(
    mode,
    m,
    sent_slot,
    tail_start,
    wide,
    deep,
    taps,
    width,
    x_ref,
    ct_ref,
    cta_ref,
    cta2_ref,
    w_ref,
    rw_ref,
    kb_ref,
    spre_ref,
    sconv_ref,
    *rest,
):
    c = lax.axis_index("chan")
    cells = wide * deep
    tail = pl.ds(tail_start, cells)
    full = mode == "full"
    if mode == "first":
        base_ref, other_ref, gs_ref, br_ref = rest
        up_ref = ct_ref.at[m]
        halo, halo2 = cta_ref[tail], cta2_ref[tail]
        own = (ct_ref[m, 0], ct_ref[m, 1])
    else:
        st_ref, st2_ref, dg_ref, dg2_ref, *rest = rest
        if full:
            hid_ref, mixed_ref, exp_in, red_in, kg_in, *rest = rest
            part_ref, up_ref, exp_ref, red_ref, kg_ref, gs_ref = rest
        else:
            base_ref, other_ref, gs_ref, br_ref, up_ref = rest
        here = pl.ds(sent_slot * cells, cells)
        last = lax.axis_index("section") == lax.axis_size("section") - 1

        mine, theirs = st_ref[here], st2_ref[here]
        own = (
            jnp.where(last, ct_ref[m, 0], jnp.where(c == 0, mine, theirs)),
            jnp.where(last, ct_ref[m, 1], jnp.where(c == 0, theirs, mine)),
        )
        for p in (0, 1):
            up_ref[p] = own[p]
        halo = jnp.where(last, cta_ref[tail], dg_ref[here])
        halo2 = jnp.where(last, cta2_ref[tail], dg2_ref[here])
    below = jnp.where(c == 0, halo2, halo)
    above = jnp.where(c == 0, halo, halo2)
    for plane, up in enumerate((below, *own, above)):
        grad = nt_dot(up, rw_ref[...]) * sconv_ref[plane]
        store_shifts(gs_ref, plane, grad.astype(BF).astype(F32), wide, deep)
    if full:
        ups2 = up_ref[...].reshape(2 * cells, LANES)
        red = jnp.dot(mixed_ref[...], ups2, preferred_element_type=F32)
        red_ref[...] = red_in[...] + red
        groups = LANES // width
        keep = diagonal_mask(width)
        left = hid_ref[...]
        right = []
        for p in (0, 1):
            parts = [
                gs_ref[p + dx, dy * deep : dy * deep + cells, :]
                for dx in range(3)
                for dy in range(3)
            ]
            right.append(jnp.concatenate(parts, axis=1))
        dense = jnp.dot(left, jnp.concatenate(right, axis=0), preferred_element_type=F32)
        for tap in range(taps):
            block = dense[:, tap * LANES : (tap + 1) * LANES].reshape(groups, width, LANES)
            thin = jnp.sum(jnp.where(keep, block, 0.0), axis=0)
            at = slice((taps - 1 - tap) * width, (taps - tap) * width)
            kg_ref[at] = kg_in[at] + thin
    planes = [(gs_ref, p) for p in range(4)]
    grads = []
    for p, grad_hidden in enumerate(conv_pairs(planes, (1,), kb_ref, cells, deep)):
        grad_pre = (grad_hidden * spre_ref[p]).astype(BF)
        branch = nt_dot(grad_pre, w_ref[...])
        if full:
            part_ref[p] = branch.astype(BF)
            grads.append(grad_pre)
        else:
            br_ref[p] = branch
    if full:
        exp_ref[...] = exp_in[...] + jnp.dot(
            x_ref[m], jnp.concatenate(grads, axis=0), preferred_element_type=F32
        )
    else:
        base_ref[...] = up_ref[c].astype(F32) + br_ref[c]
        other_ref[...] = br_ref[1 - c].astype(BF)


def emit_kernel(micro, *refs):
    ins, out_ref = refs[:-1], refs[-1]
    for m in range(micro):
        up, mine, other = ins[3 * m : 3 * m + 3]
        both = mine[...].astype(F32) + other[...].astype(F32)
        out_ref[m] = (up[...].astype(F32) + both).astype(BF)


def finish_kernel(count, scale, taps, width, *refs):
    ins, outs, thin_ref = refs[:count], refs[count:-1], refs[-1]
    total = ins[0][...].astype(F32)
    for ref in ins[1:]:
        total = total + ref[...].astype(F32)
    total = total * scale
    outs[0][...] = total[0:LANES]
    outs[1][...] = total[LANES : 2 * LANES]
    thin_ref[0 : taps * width] = total[2 * LANES :]
    for i in range(width):
        turned = thin_ref[pl.ds(i, LANES, stride=width), :].T
        outs[2][:, i] = turned[:, :taps].reshape(LANES // width, width, taps)


def SENDS(micro):
    return [[m] for m in range(micro)]


def sds(shape, dtype):
    return jax.ShapeDtypeStruct(shape, dtype)


def params(mebibytes):
    return pltpu.CompilerParams(vmem_limit_bytes=mebibytes * 2**20)


def call(kernel, name, out_shape, args, scratch=(), in_specs=None, room=16):
    vmem = pl.BlockSpec(memory_space=pltpu.VMEM)
    outs = [vmem] * len(out_shape)
    return pl.pallas_call(
        kernel,
        in_specs=[vmem] * len(args) if in_specs is None else in_specs,
        out_specs=outs,
        out_shape=out_shape,
        scratch_shapes=list(scratch),
        name=name,
        cost_estimate=pl.CostEstimate(flops=2 * 10**9, bytes_accessed=4 * 2**20, transcendentals=0),
        compiler_params=params(room),
    )(*args)


def on_device(
    section_inputs, cotangent, phase_labels, expand_weight, phase_code, kernel, reduce_weight
):
    _, micro, depth, wide, deep, trunk = section_inputs.shape
    cells = wide * deep
    taps, groups, width = kernel.shape[1], kernel.shape[2], kernel.shape[3]
    assert depth == 2 and lax.axis_size("chan") == 2
    assert trunk == LANES and groups * width == LANES
    spaces, sections = lax.axis_size("space"), lax.axis_size("section")
    scale = 1.0 / math.sqrt(micro * depth * spaces * cells)

    x = section_inputs[0].reshape(micro, depth, cells, trunk)
    ct = cotangent.reshape(micro, depth, cells, trunk)
    w, rw = expand_weight[0], reduce_weight[0]
    code = jnp.pad(phase_code[0], ((0, 8 - phase_code.shape[1]), (0, 0)))
    kern = kernel[0].transpose(1, 2, 3, 0)

    away = [(k, c, (k + 2 * c - 1) % spaces) for k in range(spaces) for c in (0, 1)]
    back = [(k, c, (k - 2 * c + 1) % spaces) for k in range(spaces) for c in (0, 1)]
    route_a = [(2 * k + c, 2 * t + c) for k, c, t in away]
    route_b = [(2 * k + c, 2 * t + c) for k, c, t in back]
    route_d = [
        ((k * sections + s) * 2 + c, (t * sections + (s - 1) % sections) * 2 + c)
        for k, c, t in away
        for s in range(sections)
    ]
    route_s = [(s, (s - 1) % sections) for s in range(sections)]

    def swap(v):
        return lax.ppermute(v, "chan", [(0, 1), (1, 0)])

    rows = cells + wide
    hbm = pl.BlockSpec(memory_space=pltpu.HBM)
    packed_a, packed_b, lab = call(
        functools.partial(pack_kernel, micro, cells, wide),
        "pack",
        [
            sds((micro * rows + cells, LANES), BF),
            sds((micro * rows, LANES), BF),
            sds((micro, depth, deep, LANES), BF),
        ],
        (x, ct, phase_labels),
        [
            pltpu.VMEM(phase_labels.shape, jnp.int32),
            pltpu.SemaphoreType.DMA((2 * micro + 2,)),
        ],
        [hbm, hbm, hbm],
        60,
    )
    plane2, plane4, flat = (2, cells, LANES), (4, cells, LANES), (cells, LANES)
    pad_rows = cells + 2 * deep
    square, thin = (LANES, LANES), (taps * width, LANES)
    dense_f, dense_b = call(
        functools.partial(weights_kernel, taps, width),
        "weights",
        [sds((4 * taps // 3 * LANES, 2 * LANES), BF)] * 2,
        (kern,),
        [pltpu.VMEM((LANES * width, LANES), F32), pltpu.VMEM((2,) + thin, F32)],
    )
    *owned, x, ct, w, rw, code, edge, flip = call(
        functools.partial(own_kernel, micro, wide, deep),
        "own",
        [sds((2, pad_rows, 3 * LANES), BF), sds((LANES, 2 * cells), BF), sds(plane2, F32)]
        * micro
        + [sds(v.shape, v.dtype) for v in (x, ct, w, rw, code)]
        + [sds((max(1, micro - 1) * cells, LANES), BF), sds((micro, LANES, 2 * cells), BF)],
        (x, ct, lab, w, rw, code),
    )
    a = lax.ppermute(packed_a, ("space", "chan"), route_a)
    b = lax.ppermute(packed_b, ("space", "chan"), route_b)
    a, b, dense_f, dense_b, *owned = lax.optimization_barrier((a, b, dense_f, dense_b, *owned))
    halos = (a, b, swap(a), swap(b))
    edge = lax.ppermute(edge, ("space", "chan"), route_a)

    def joined(pairs):
        outs = [(base + swap(other).astype(F32)).astype(BF) for base, other in pairs]
        return outs[0] if len(outs) == 1 else jnp.concatenate(outs, axis=0)

    def send_on(out):
        st = lax.ppermute(out, "section", route_s)
        dg = lax.ppermute(out, ("space", "section", "chan"), route_d)
        return st, dg

    def after(arrays, first):
        *arrays, _ = lax.optimization_barrier((*arrays, first))
        return arrays

    def shared(st, dg):
        return st, swap(st), dg, swap(dg)

    def back_pass(mode, m, extra, extra_out=()):
        outs = [sds(flat, F32), sds(flat, BF)] if mode != "full" else [sds(plane2, BF)] * 2
        scratch = [pltpu.VMEM((4, pad_rows, 3 * LANES), BF)]
        if mode != "full":
            scratch.append(pltpu.VMEM(plane2, F32))
        if mode == "light":
            scratch.append(pltpu.VMEM(plane2, BF))
        return call(
            functools.partial(backward_kernel, mode, m, sent_slot[m], tails[m], wide, deep, taps, width),
            "backward_" + mode,
            outs + list(extra_out),
            (flip, ct, *edges[m], w, rw, dense_b, spre[m], sconv[m], *extra),
            scratch,
        )

    sconv, mixed, sent = [], [], []
    sends = SENDS(micro)
    sender = [n for n, group in enumerate(sends) for _ in group]
    sent_slot = [i for group in sends for i in range(len(group))]
    spre = [owned[3 * m + 2] for m in range(micro)]
    tails = [micro * rows] + [m * cells for m in range(micro - 1)]
    edges = [(halos[0], halos[2])]
    pending, previous = [], None
    for m in range(micro):
        con, mix = call(
            functools.partial(forward_kernel, m, wide, deep),
            "forward",
            [sds(plane4, F32), sds((LANES, 2 * cells), BF)],
            (owned[3 * m], *halos, w, code, dense_f),
            [pltpu.VMEM((4, pad_rows, 3 * LANES), BF)],
        )
        sconv.append(con)
        mixed.append(mix)
        (code,) = after((code,), con)
        if m == 0:
            previous = back_pass("first", 0, ())
            (code,) = after((code,), previous[1])
            sent.append(send_on(joined([previous])))
    (edge,) = after((edge,), sconv[-1])
    edges += [(edge, swap(edge))] * (micro - 1)
    for m in range(1, micro):
        (sconv[m],) = after((sconv[m],), previous[1])
        previous = back_pass("first", m, ())
        sent.append(send_on(joined([previous])))
    sent[0] = after(sent[0], previous[1])
    ups = [shared(*pair) for pair in sent]

    rank = lax.axis_index("section")
    for stage in range(1, sections - 1):
        fresh = []
        for group in sends:
            out = joined([back_pass("light", m, ups[sender[m]]) for m in group])
            fresh.append(shared(*send_on(out)))
        mine = rank == sections - 2 - stage
        ups = [
            tuple(jnp.where(mine, n, o) for n, o in zip(new, old)) for new, old in zip(fresh, ups)
        ]
    sum_shapes = [sds(s, F32) for s in (square, square, thin)]
    sums = [jnp.zeros(s.shape, F32) for s in sum_shapes]
    pieces = []
    for m in range(micro):
        extra = (*ups[sender[m]], owned[3 * m + 1], mixed[m], *sums)
        part, up, *sums = back_pass("full", m, extra, sum_shapes)
        if m == 0 and sections == 2 and sender[-1] > 0:
            ups[-1] = shared(*after(sent[-1], part))
        pieces += [up, part, swap(part)]

    grads = jnp.concatenate([s.astype(BF) for s in sums], axis=0)
    if spaces == 4:
        near = [(k, k ^ 1) for k in range(spaces)]
        far = [(k, k ^ 3) for k in range(spaces)]
        grads = grads + lax.ppermute(grads, "space", near)
        copies = [grads, lax.ppermute(grads, "space", far)]
    else:
        copies = [lax.psum(grads, "space")]
    (out,) = call(
        functools.partial(emit_kernel, micro), "emit", [sds((micro,) + plane2, BF)], pieces
    )
    *copies, out = lax.optimization_barrier((*copies, out))
    exp_g, red_g, kg = call(
        functools.partial(finish_kernel, len(copies), scale, taps, width),
        "finish",
        [sds(square, F32), sds(square, F32), sds((groups, width, width, taps), F32)],
        copies,
        [pltpu.VMEM((LANES * width, LANES), F32)],
    )
    kg = kg.transpose(3, 0, 1, 2)
    return (
        out.reshape(section_inputs.shape),
        exp_g[None],
        kg[None],
        red_g[None],
    )


def solution(mesh):
    placed = (
        P("section", "parts", "space", None, None, None),
        P("parts", "space", None, None, None),
        P("parts", "space", None, None),
        P("section", None, "chan"),
        P("section", None, "chan"),
        P("section", None, "chan", None, None),
        P("section", "chan", None),
    )
    return jax.shard_map(
        on_device,
        mesh=mesh,
        in_specs=placed,
        out_specs=(
            P("section", "parts", "space", None, None, None),
            P(("parts", "section"), None, "chan"),
            P(("parts", "section"), None, "chan", None, None),
            P(("parts", "section"), "chan", None),
        ),
        check_vma=False,
    )
```

```python
import functools
import math

import jax
import jax.numpy as jnp
from jax import lax
from jax.experimental import pallas as pl
from jax.experimental.pallas import tpu as pltpu
from jax.sharding import PartitionSpec as P

BF = jnp.bfloat16
F32 = jnp.float32
LANES = 128


def gate(v):
    return 0.5 + 0.5 * jnp.tanh(0.5 * v)


def slope(v, q):
    return q * (1.0 + v * (1.0 - q))


def nt_dot(a, b):
    return lax.dot_general(a, b, (((1,), (1,)), ((), ())), preferred_element_type=F32)


def store_shifts(ref, plane, value, wide, deep):
    cells = wide * deep
    cube = value.reshape(wide, deep, LANES)
    for j, turn in enumerate((1, 0, deep - 1)):
        moved = cube if turn == 0 else pltpu.roll(cube, turn, axis=1)
        flat = moved.reshape(cells, LANES).astype(BF)
        lanes = slice(j * LANES, (j + 1) * LANES)
        ref[plane, deep : deep + cells, lanes] = flat
        ref[plane, 0:deep, lanes] = flat[cells - deep :]
        ref[plane, deep + cells : cells + 2 * deep, lanes] = flat[:deep]


def pair_rows(planes, first, cells, deep):
    parts = []
    for at in range(first - 1, first + 3):
        ref, plane = planes[at]
        for dy in range(3):
            parts.append(ref[plane, dy * deep : dy * deep + cells, :])
    return jnp.concatenate(parts, axis=1)


def conv_pairs(planes, firsts, weights, cells, deep):
    rows = [pair_rows(planes, first, cells, deep) for first in firsts]
    rows = rows[0] if len(rows) == 1 else jnp.concatenate(rows, axis=0)
    both = jnp.dot(rows, weights[...], preferred_element_type=F32)
    outs = []
    for n in range(len(firsts)):
        for o in range(2):
            outs.append(both[n * cells : (n + 1) * cells, o * LANES : (o + 1) * LANES])
    return outs


def pack_kernel(
    micro, cells, wide, x_ref, ct_ref, tag_ref, a_ref, b_ref, own_ref, lab_ref, sem
):
    tags = pltpu.make_async_copy(tag_ref, lab_ref, sem.at[2 * micro + 1])
    tags.start()
    c = lax.axis_index("chan")
    copies = []
    for m in range(micro):
        for n, out_ref in enumerate((a_ref, b_ref)):
            spot = out_ref.at[pl.ds(m * (cells + wide), cells)]
            copy = pltpu.make_async_copy(x_ref.at[m, c], spot, sem.at[2 * m + n])
            copy.start()
            copies.append(copy)
    spot = a_ref.at[pl.ds(micro * (cells + wide), cells)]
    copy = pltpu.make_async_copy(ct_ref.at[0, c], spot, sem.at[2 * micro])
    copy.start()
    copies.append(copy)
    deep = lab_ref.shape[3]
    tags.wait()
    row = lax.broadcasted_iota(jnp.int32, (LANES, LANES), 0)
    lane = lax.broadcasted_iota(jnp.int32, (LANES, LANES), 1)
    eye = jnp.where(row == lane, 1.0, 0.0)[:deep, :deep].astype(BF)
    for m in range(micro):
        for p in range(2):
            own_ref[m, p] = jnp.zeros((deep, LANES), BF)
            turned = nt_dot(eye, lab_ref[m, p].astype(F32).astype(BF))
            own_ref[m, p, :, 0:wide] = turned.astype(BF)
        for out_ref in (a_ref, b_ref):
            out_ref[m * (cells + wide) + cells : (m + 1) * (cells + wide)] = own_ref[m, c]
    for copy in copies:
        copy.wait()


def diagonal_mask(width):
    groups = LANES // width
    g = lax.broadcasted_iota(jnp.int32, (groups, width, LANES), 0)
    lane = lax.broadcasted_iota(jnp.int32, (groups, width, LANES), 2)
    return g == lane // width


def weights_kernel(taps, width, k_ref, f_ref, b_ref, flat_ref, thin_ref):
    groups = LANES // width
    keep = diagonal_mask(width)
    flat_ref[:, 0:taps] = k_ref[...].astype(F32).reshape(groups * width * width, taps)
    for i in range(width):
        rows = [
            flat_ref[(g * width + i) * width : (g * width + i + 1) * width, :]
            for g in range(groups)
        ]
        turned = jnp.concatenate(rows, axis=0).T
        thin_ref[0, pl.ds(i, taps, stride=width), :] = turned[:taps]
        turned = flat_ref[pl.ds(i, LANES, stride=width), :].T
        thin_ref[1, pl.ds(i, taps, stride=width), :] = turned[:taps]
    third = taps // 3 * LANES
    zero = jnp.zeros((third, LANES), BF)
    for n, dst in enumerate((f_ref, b_ref)):
        dst[0:third, LANES:] = zero
        dst[3 * third :, 0:LANES] = zero
        for t in range(taps):
            one = thin_ref[n, t * width : (t + 1) * width, :]
            full = jnp.where(keep, jnp.broadcast_to(one[None], keep.shape), 0.0)
            full = full.reshape(LANES, LANES).astype(BF)
            at = (t if n == 0 else taps - 1 - t) * LANES
            dst[at : at + LANES, 0:LANES] = full
            dst[third + at : third + at + LANES, LANES:] = full


def hidden_rows(x, lab, w, codes, wide, deep):
    pre = jnp.dot(x, w, preferred_element_type=F32)
    lab = lab.astype(F32)
    adds = []
    for y in range(wide):
        tag = jnp.broadcast_to(lab[:, y : y + 1], (deep, LANES))
        adds.append(jnp.where(tag < 0.5, codes[0], jnp.where(tag < 1.5, codes[1], codes[2])))
    return pre + jnp.concatenate(adds, axis=0)


def code_rows(code_ref, deep):
    return [jnp.broadcast_to(code_ref[i : i + 1, :], (deep, LANES)) for i in range(3)]


def own_kernel(
    micro, wide, deep, x_ref, ct_ref, lab_ref, w_ref, rw_ref, code_ref, *outs
):
    *kept, edge_ref, flip_ref = outs[3 * micro :]
    for src, dst in zip((x_ref, ct_ref, w_ref, rw_ref, code_ref), kept):
        dst[...] = src[...]
    c = lax.axis_index("chan")
    cells = wide * deep
    for m in range(1, micro):
        edge_ref[(m - 1) * cells : m * cells] = ct_ref[m, c]
    codes = code_rows(code_ref, deep)
    for m in range(micro):
        hs_ref, hid_ref, spre_ref = outs[3 * m : 3 * m + 3]
        flip_ref[m] = x_ref[m].reshape(2 * cells, LANES).T
        for p in range(2):
            pre = hidden_rows(x_ref[m, p], lab_ref[m, p], w_ref[...], codes, wide, deep)
            q = gate(pre)
            h = pre * q
            hid_ref[:, p * cells : (p + 1) * cells] = h.astype(BF).T
            spre_ref[p] = slope(pre, q)
            store_shifts(hs_ref, p, h, wide, deep)


def forward_kernel(
    slot,
    wide,
    deep,
    own_ref,
    a_ref,
    b_ref,
    a2_ref,
    b2_ref,
    w_ref,
    code_ref,
    kf_ref,
    sconv_ref,
    mixed_ref,
    hs_ref,
):
    c = lax.axis_index("chan")
    cells = wide * deep
    codes = code_rows(code_ref, deep)
    start = slot * (cells + wide)
    first = c == 0
    sources = ((b_ref, b2_ref), (a2_ref, a_ref), (a_ref, a2_ref), (b2_ref, b_ref))
    for plane, (yes, no) in enumerate(sources):
        rows = slice(start, start + cells + wide)
        both = jnp.where(first, yes[rows], no[rows])
        pre = hidden_rows(both[:cells], both[cells:], w_ref[...], codes, wide, deep)
        store_shifts(hs_ref, plane, pre * gate(pre), wide, deep)
    planes = [(hs_ref, 0), (hs_ref, 1), (own_ref, 0), (own_ref, 1), (hs_ref, 2), (hs_ref, 3)]
    for p, conv in enumerate(conv_pairs(planes, (1, 3), kf_ref, cells, deep)):
        q = gate(conv)
        sconv_ref[p] = slope(conv, q)
        if p in (1, 2):
            mixed_ref[:, (p - 1) * cells : p * cells] = (conv * q).astype(BF).T


def backward_kernel(
    mode,
    m,
    sent_slot,
    tail_start,
    wide,
    deep,
    taps,
    width,
    x_ref,
    ct_ref,
    cta_ref,
    cta2_ref,
    w_ref,
    rw_ref,
    kb_ref,
    spre_ref,
    sconv_ref,
    *rest,
):
    c = lax.axis_index("chan")
    cells = wide * deep
    tail = pl.ds(tail_start, cells)
    full = mode == "full"
    if mode == "first":
        base_ref, other_ref, gs_ref, br_ref = rest
        up_ref = ct_ref.at[m]
        halo, halo2 = cta_ref[tail], cta2_ref[tail]
        own = (ct_ref[m, 0], ct_ref[m, 1])
    else:
        st_ref, st2_ref, dg_ref, dg2_ref, *rest = rest
        if full:
            hid_ref, mixed_ref, exp_in, red_in, kg_in, *rest = rest
            part_ref, up_ref, exp_ref, red_ref, kg_ref, gs_ref = rest
        else:
            base_ref, other_ref, gs_ref, br_ref, up_ref = rest
        here = pl.ds(sent_slot * cells, cells)
        last = lax.axis_index("section") == lax.axis_size("section") - 1

        mine, theirs = st_ref[here], st2_ref[here]
        own = (
            jnp.where(last, ct_ref[m, 0], jnp.where(c == 0, mine, theirs)),
            jnp.where(last, ct_ref[m, 1], jnp.where(c == 0, theirs, mine)),
        )
        for p in (0, 1):
            up_ref[p] = own[p]
        halo = jnp.where(last, cta_ref[tail], dg_ref[here])
        halo2 = jnp.where(last, cta2_ref[tail], dg2_ref[here])
    below = jnp.where(c == 0, halo2, halo)
    above = jnp.where(c == 0, halo, halo2)
    for plane, up in enumerate((below, *own, above)):
        grad = nt_dot(up, rw_ref[...]) * sconv_ref[plane]
        store_shifts(gs_ref, plane, grad.astype(BF).astype(F32), wide, deep)
    if full:
        ups2 = up_ref[...].reshape(2 * cells, LANES)
        red = jnp.dot(mixed_ref[...], ups2, preferred_element_type=F32)
        red_ref[...] = red_in[...] + red
        groups = LANES // width
        keep = diagonal_mask(width)
        left = hid_ref[...]
        right = []
        for p in (0, 1):
            parts = [
                gs_ref[p + dx, dy * deep : dy * deep + cells, :]
                for dx in range(3)
                for dy in range(3)
            ]
            right.append(jnp.concatenate(parts, axis=1))
        dense = jnp.dot(left, jnp.concatenate(right, axis=0), preferred_element_type=F32)
        for tap in range(taps):
            block = dense[:, tap * LANES : (tap + 1) * LANES].reshape(groups, width, LANES)
            thin = jnp.sum(jnp.where(keep, block, 0.0), axis=0)
            at = slice((taps - 1 - tap) * width, (taps - tap) * width)
            kg_ref[at] = kg_in[at] + thin
    planes = [(gs_ref, p) for p in range(4)]
    grads = []
    for p, grad_hidden in enumerate(conv_pairs(planes, (1,), kb_ref, cells, deep)):
        grad_pre = (grad_hidden * spre_ref[p]).astype(BF)
        branch = nt_dot(grad_pre, w_ref[...])
        if full:
            part_ref[p] = branch.astype(BF)
            grads.append(grad_pre)
        else:
            br_ref[p] = branch
    if full:
        exp_ref[...] = exp_in[...] + jnp.dot(
            x_ref[m], jnp.concatenate(grads, axis=0), preferred_element_type=F32
        )
    else:
        base_ref[...] = up_ref[c].astype(F32) + br_ref[c]
        other_ref[...] = br_ref[1 - c].astype(BF)


def emit_kernel(micro, *refs):
    ins, out_ref = refs[:-1], refs[-1]
    for m in range(micro):
        up, mine, other = ins[3 * m : 3 * m + 3]
        both = mine[...].astype(F32) + other[...].astype(F32)
        out_ref[m] = (up[...].astype(F32) + both).astype(BF)


def finish_kernel(count, scale, taps, width, *refs):
    ins, outs, thin_ref = refs[:count], refs[count:-1], refs[-1]
    total = ins[0][...].astype(F32)
    for ref in ins[1:]:
        total = total + ref[...].astype(F32)
    total = total * scale
    outs[0][...] = total[0:LANES]
    outs[1][...] = total[LANES : 2 * LANES]
    thin_ref[0 : taps * width] = total[2 * LANES :]
    for i in range(width):
        turned = thin_ref[pl.ds(i, LANES, stride=width), :].T
        outs[2][:, i] = turned[:, :taps].reshape(LANES // width, width, taps)


def SENDS(micro):
    return [[0], list(range(1, micro))] if micro > 1 else [[0]]


def sds(shape, dtype):
    return jax.ShapeDtypeStruct(shape, dtype)


def params(mebibytes):
    return pltpu.CompilerParams(vmem_limit_bytes=mebibytes * 2**20)


def call(kernel, name, out_shape, args, scratch=(), in_specs=None, room=16):
    vmem = pl.BlockSpec(memory_space=pltpu.VMEM)
    outs = [vmem] * len(out_shape)
    return pl.pallas_call(
        kernel,
        in_specs=[vmem] * len(args) if in_specs is None else in_specs,
        out_specs=outs,
        out_shape=out_shape,
        scratch_shapes=list(scratch),
        name=name,
        cost_estimate=pl.CostEstimate(flops=2 * 10**9, bytes_accessed=4 * 2**20, transcendentals=0),
        compiler_params=params(room),
    )(*args)


def on_device(
    section_inputs, cotangent, phase_labels, expand_weight, phase_code, kernel, reduce_weight
):
    _, micro, depth, wide, deep, trunk = section_inputs.shape
    cells = wide * deep
    taps, groups, width = kernel.shape[1], kernel.shape[2], kernel.shape[3]
    assert depth == 2 and lax.axis_size("chan") == 2
    assert trunk == LANES and groups * width == LANES
    spaces, sections = lax.axis_size("space"), lax.axis_size("section")
    scale = 1.0 / math.sqrt(micro * depth * spaces * cells)

    x = section_inputs[0].reshape(micro, depth, cells, trunk)
    ct = cotangent.reshape(micro, depth, cells, trunk)
    w, rw = expand_weight[0], reduce_weight[0]
    code = jnp.pad(phase_code[0], ((0, 8 - phase_code.shape[1]), (0, 0)))
    kern = kernel[0].transpose(1, 2, 3, 0)

    away = [(k, c, (k + 2 * c - 1) % spaces) for k in range(spaces) for c in (0, 1)]
    back = [(k, c, (k - 2 * c + 1) % spaces) for k in range(spaces) for c in (0, 1)]
    route_a = [(2 * k + c, 2 * t + c) for k, c, t in away]
    route_b = [(2 * k + c, 2 * t + c) for k, c, t in back]
    route_d = [
        ((k * sections + s) * 2 + c, (t * sections + (s - 1) % sections) * 2 + c)
        for k, c, t in away
        for s in range(sections)
    ]
    route_s = [(s, (s - 1) % sections) for s in range(sections)]

    def swap(v):
        return lax.ppermute(v, "chan", [(0, 1), (1, 0)])

    rows = cells + wide
    hbm = pl.BlockSpec(memory_space=pltpu.HBM)
    packed_a, packed_b, lab = call(
        functools.partial(pack_kernel, micro, cells, wide),
        "pack",
        [
            sds((micro * rows + cells, LANES), BF),
            sds((micro * rows, LANES), BF),
            sds((micro, depth, deep, LANES), BF),
        ],
        (x, ct, phase_labels),
        [
            pltpu.VMEM(phase_labels.shape, jnp.int32),
            pltpu.SemaphoreType.DMA((2 * micro + 2,)),
        ],
        [hbm, hbm, hbm],
        60,
    )
    plane2, plane4, flat = (2, cells, LANES), (4, cells, LANES), (cells, LANES)
    pad_rows = cells + 2 * deep
    square, thin = (LANES, LANES), (taps * width, LANES)
    dense_f, dense_b = call(
        functools.partial(weights_kernel, taps, width),
        "weights",
        [sds((4 * taps // 3 * LANES, 2 * LANES), BF)] * 2,
        (kern,),
        [pltpu.VMEM((LANES * width, LANES), F32), pltpu.VMEM((2,) + thin, F32)],
    )
    *owned, x, ct, w, rw, code, edge, flip = call(
        functools.partial(own_kernel, micro, wide, deep),
        "own",
        [sds((2, pad_rows, 3 * LANES), BF), sds((LANES, 2 * cells), BF), sds(plane2, F32)]
        * micro
        + [sds(v.shape, v.dtype) for v in (x, ct, w, rw, code)]
        + [sds((max(1, micro - 1) * cells, LANES), BF), sds((micro, LANES, 2 * cells), BF)],
        (x, ct, lab, w, rw, code),
    )
    a = lax.ppermute(packed_a, ("space", "chan"), route_a)
    b = lax.ppermute(packed_b, ("space", "chan"), route_b)
    a, b, dense_f, dense_b, *owned = lax.optimization_barrier((a, b, dense_f, dense_b, *owned))
    halos = (a, b, swap(a), swap(b))
    edge = lax.ppermute(edge, ("space", "chan"), route_a)

    def joined(pairs):
        outs = [(base + swap(other).astype(F32)).astype(BF) for base, other in pairs]
        return outs[0] if len(outs) == 1 else jnp.concatenate(outs, axis=0)

    def send_on(out):
        st = lax.ppermute(out, "section", route_s)
        dg = lax.ppermute(out, ("space", "section", "chan"), route_d)
        return st, dg

    def after(arrays, first):
        *arrays, _ = lax.optimization_barrier((*arrays, first))
        return arrays

    def shared(st, dg):
        return st, swap(st), dg, swap(dg)

    def back_pass(mode, m, extra, extra_out=()):
        outs = [sds(flat, F32), sds(flat, BF)] if mode != "full" else [sds(plane2, BF)] * 2
        scratch = [pltpu.VMEM((4, pad_rows, 3 * LANES), BF)]
        if mode != "full":
            scratch.append(pltpu.VMEM(plane2, F32))
        if mode == "light":
            scratch.append(pltpu.VMEM(plane2, BF))
        return call(
            functools.partial(backward_kernel, mode, m, sent_slot[m], tails[m], wide, deep, taps, width),
            "backward_" + mode,
            outs + list(extra_out),
            (flip, ct, *edges[m], w, rw, dense_b, spre[m], sconv[m], *extra),
            scratch,
        )

    sconv, mixed, sent = [], [], []
    sends = SENDS(micro)
    sender = [n for n, group in enumerate(sends) for _ in group]
    sent_slot = [i for group in sends for i in range(len(group))]
    spre = [owned[3 * m + 2] for m in range(micro)]
    tails = [micro * rows] + [m * cells for m in range(micro - 1)]
    edges = [(halos[0], halos[2])]
    pending, previous = [], None
    for m in range(micro):
        con, mix = call(
            functools.partial(forward_kernel, m, wide, deep),
            "forward",
            [sds(plane4, F32), sds((LANES, 2 * cells), BF)],
            (owned[3 * m], *halos, w, code, dense_f),
            [pltpu.VMEM((4, pad_rows, 3 * LANES), BF)],
        )
        sconv.append(con)
        mixed.append(mix)
        (code,) = after((code,), con)
        if m == 0:
            previous = back_pass("first", 0, ())
            (code,) = after((code,), previous[1])
            sent.append(send_on(joined([previous])))
    (edge,) = after((edge,), sconv[-1])
    edges += [(edge, swap(edge))] * (micro - 1)
    waiting = []
    for m in range(1, micro):
        (sconv[m],) = after((sconv[m],), previous[1])
        previous = back_pass("first", m, ())
        waiting.append(previous)
    sent.append(send_on(joined(waiting)))
    sent[0] = after(sent[0], previous[1])
    ups = [shared(*pair) for pair in sent]

    rank = lax.axis_index("section")
    for stage in range(1, sections - 1):
        fresh = []
        for group in sends:
            out = joined([back_pass("light", m, ups[sender[m]]) for m in group])
            fresh.append(shared(*send_on(out)))
        mine = rank == sections - 2 - stage
        ups = [
            tuple(jnp.where(mine, n, o) for n, o in zip(new, old)) for new, old in zip(fresh, ups)
        ]
    sum_shapes = [sds(s, F32) for s in (square, square, thin)]
    sums = [jnp.zeros(s.shape, F32) for s in sum_shapes]
    pieces = []
    for m in range(micro):
        extra = (*ups[sender[m]], owned[3 * m + 1], mixed[m], *sums)
        part, up, *sums = back_pass("full", m, extra, sum_shapes)
        if m == 0 and sections == 2 and sender[-1] > 0:
            ups[-1] = shared(*after(sent[-1], part))
        pieces += [up, part, swap(part)]

    grads = jnp.concatenate([s.astype(BF) for s in sums], axis=0)
    if spaces == 4:
        near = [(k, k ^ 1) for k in range(spaces)]
        far = [(k, k ^ 3) for k in range(spaces)]
        grads = grads + lax.ppermute(grads, "space", near)
        copies = [grads, lax.ppermute(grads, "space", far)]
    else:
        copies = [lax.psum(grads, "space")]
    (out,) = call(
        functools.partial(emit_kernel, micro), "emit", [sds((micro,) + plane2, BF)], pieces
    )
    *copies, out = lax.optimization_barrier((*copies, out))
    exp_g, red_g, kg = call(
        functools.partial(finish_kernel, len(copies), scale, taps, width),
        "finish",
        [sds(square, F32), sds(square, F32), sds((groups, width, width, taps), F32)],
        copies,
        [pltpu.VMEM((LANES * width, LANES), F32)],
    )
    kg = kg.transpose(3, 0, 1, 2)
    return (
        out.reshape(section_inputs.shape),
        exp_g[None],
        kg[None],
        red_g[None],
    )


def solution(mesh):
    placed = (
        P("section", "parts", "space", None, None, None),
        P("parts", "space", None, None, None),
        P("parts", "space", None, None),
        P("section", None, "chan"),
        P("section", None, "chan"),
        P("section", None, "chan", None, None),
        P("section", "chan", None),
    )
    return jax.shard_map(
        on_device,
        mesh=mesh,
        in_specs=placed,
        out_specs=(
            P("section", "parts", "space", None, None, None),
            P(("parts", "section"), None, "chan"),
            P(("parts", "section"), None, "chan", None, None),
            P(("parts", "section"), "chan", None),
        ),
        check_vma=False,
    )
```

```python
import functools
import math

import jax
import jax.numpy as jnp
from jax import lax
from jax.experimental import pallas as pl
from jax.experimental.pallas import tpu as pltpu
from jax.sharding import PartitionSpec as P

BF = jnp.bfloat16
F32 = jnp.float32
LANES = 128


def gate(v):
    return 0.5 + 0.5 * jnp.tanh(0.5 * v)


def slope(v, q):
    return q * (1.0 + v * (1.0 - q))


def nt_dot(a, b):
    return lax.dot_general(a, b, (((1,), (1,)), ((), ())), preferred_element_type=F32)


def store_shifts(ref, plane, value, wide, deep):
    cells = wide * deep
    cube = value.reshape(wide, deep, LANES)
    for j, turn in enumerate((1, 0, deep - 1)):
        moved = cube if turn == 0 else pltpu.roll(cube, turn, axis=1)
        flat = moved.reshape(cells, LANES).astype(BF)
        lanes = slice(j * LANES, (j + 1) * LANES)
        ref[plane, deep : deep + cells, lanes] = flat
        ref[plane, 0:deep, lanes] = flat[cells - deep :]
        ref[plane, deep + cells : cells + 2 * deep, lanes] = flat[:deep]


def pair_rows(planes, first, cells, deep):
    parts = []
    for at in range(first - 1, first + 3):
        ref, plane = planes[at]
        for dy in range(3):
            parts.append(ref[plane, dy * deep : dy * deep + cells, :])
    return jnp.concatenate(parts, axis=1)


def conv_pairs(planes, firsts, weights, cells, deep):
    rows = [pair_rows(planes, first, cells, deep) for first in firsts]
    rows = rows[0] if len(rows) == 1 else jnp.concatenate(rows, axis=0)
    both = jnp.dot(rows, weights[...], preferred_element_type=F32)
    outs = []
    for n in range(len(firsts)):
        for o in range(2):
            outs.append(both[n * cells : (n + 1) * cells, o * LANES : (o + 1) * LANES])
    return outs


def pack_kernel(
    micro, cells, wide, x_ref, ct_ref, tag_ref, a_ref, b_ref, own_ref, lab_ref, sem
):
    tags = pltpu.make_async_copy(tag_ref, lab_ref, sem.at[2 * micro + 1])
    tags.start()
    c = lax.axis_index("chan")
    copies = []
    for m in range(micro):
        spot = a_ref.at[pl.ds(m * (cells + wide), cells)]
        copy = pltpu.make_async_copy(x_ref.at[m, c], spot, sem.at[m])
        copy.start()
        copies.append(copy)
    spot = a_ref.at[pl.ds(micro * (cells + wide), cells)]
    copy = pltpu.make_async_copy(ct_ref.at[0, c], spot, sem.at[2 * micro])
    copy.start()
    copies.append(copy)
    deep = lab_ref.shape[3]
    tags.wait()
    row = lax.broadcasted_iota(jnp.int32, (LANES, LANES), 0)
    lane = lax.broadcasted_iota(jnp.int32, (LANES, LANES), 1)
    eye = jnp.where(row == lane, 1.0, 0.0)[:deep, :deep].astype(BF)
    for m in range(micro):
        for p in range(2):
            own_ref[m, p] = jnp.zeros((deep, LANES), BF)
            turned = nt_dot(eye, lab_ref[m, p].astype(F32).astype(BF))
            own_ref[m, p, :, 0:wide] = turned.astype(BF)
        for out_ref in (a_ref, b_ref):
            out_ref[m * (cells + wide) + cells : (m + 1) * (cells + wide)] = own_ref[m, c]
    for copy in copies:
        copy.wait()
    for m in range(micro):
        rows = slice(m * (cells + wide), m * (cells + wide) + cells)
        b_ref[rows] = a_ref[rows]


def diagonal_mask(width):
    groups = LANES // width
    g = lax.broadcasted_iota(jnp.int32, (groups, width, LANES), 0)
    lane = lax.broadcasted_iota(jnp.int32, (groups, width, LANES), 2)
    return g == lane // width


def weights_kernel(taps, width, k_ref, f_ref, b_ref, flat_ref, thin_ref):
    groups = LANES // width
    keep = diagonal_mask(width)
    flat_ref[:, 0:taps] = k_ref[...].astype(F32).reshape(groups * width * width, taps)
    for i in range(width):
        rows = [
            flat_ref[(g * width + i) * width : (g * width + i + 1) * width, :]
            for g in range(groups)
        ]
        turned = jnp.concatenate(rows, axis=0).T
        thin_ref[0, pl.ds(i, taps, stride=width), :] = turned[:taps]
        turned = flat_ref[pl.ds(i, LANES, stride=width), :].T
        thin_ref[1, pl.ds(i, taps, stride=width), :] = turned[:taps]
    third = taps // 3 * LANES
    zero = jnp.zeros((third, LANES), BF)
    for n, dst in enumerate((f_ref, b_ref)):
        dst[0:third, LANES:] = zero
        dst[3 * third :, 0:LANES] = zero
        for t in range(taps):
            one = thin_ref[n, t * width : (t + 1) * width, :]
            full = jnp.where(keep, jnp.broadcast_to(one[None], keep.shape), 0.0)
            full = full.reshape(LANES, LANES).astype(BF)
            at = (t if n == 0 else taps - 1 - t) * LANES
            dst[at : at + LANES, 0:LANES] = full
            dst[third + at : third + at + LANES, LANES:] = full


def hidden_rows(x, lab, w, codes, wide, deep):
    pre = jnp.dot(x, w, preferred_element_type=F32)
    lab = lab.astype(F32)
    adds = []
    for y in range(wide):
        tag = jnp.broadcast_to(lab[:, y : y + 1], (deep, LANES))
        adds.append(jnp.where(tag < 0.5, codes[0], jnp.where(tag < 1.5, codes[1], codes[2])))
    return pre + jnp.concatenate(adds, axis=0)


def code_rows(code_ref, deep):
    return [jnp.broadcast_to(code_ref[i : i + 1, :], (deep, LANES)) for i in range(3)]


def own_kernel(
    micro, wide, deep, x_ref, ct_ref, lab_ref, w_ref, rw_ref, code_ref, *outs
):
    *kept, edge_ref, flip_ref = outs[3 * micro :]
    for src, dst in zip((x_ref, ct_ref, w_ref, rw_ref, code_ref), kept):
        dst[...] = src[...]
    c = lax.axis_index("chan")
    cells = wide * deep
    for m in range(1, micro):
        edge_ref[(m - 1) * cells : m * cells] = ct_ref[m, c]
    codes = code_rows(code_ref, deep)
    for m in range(micro):
        hs_ref, hid_ref, spre_ref = outs[3 * m : 3 * m + 3]
        flip_ref[m] = x_ref[m].reshape(2 * cells, LANES).T
        for p in range(2):
            pre = hidden_rows(x_ref[m, p], lab_ref[m, p], w_ref[...], codes, wide, deep)
            q = gate(pre)
            h = pre * q
            hid_ref[:, p * cells : (p + 1) * cells] = h.astype(BF).T
            spre_ref[p] = slope(pre, q)
            store_shifts(hs_ref, p, h, wide, deep)


def forward_kernel(
    slot,
    wide,
    deep,
    own_ref,
    a_ref,
    b_ref,
    a2_ref,
    b2_ref,
    w_ref,
    code_ref,
    kf_ref,
    sconv_ref,
    mixed_ref,
    hs_ref,
):
    c = lax.axis_index("chan")
    cells = wide * deep
    codes = code_rows(code_ref, deep)
    start = slot * (cells + wide)
    first = c == 0
    sources = ((b_ref, b2_ref), (a2_ref, a_ref), (a_ref, a2_ref), (b2_ref, b_ref))
    for plane, (yes, no) in enumerate(sources):
        rows = slice(start, start + cells + wide)
        both = jnp.where(first, yes[rows], no[rows])
        pre = hidden_rows(both[:cells], both[cells:], w_ref[...], codes, wide, deep)
        store_shifts(hs_ref, plane, pre * gate(pre), wide, deep)
    planes = [(hs_ref, 0), (hs_ref, 1), (own_ref, 0), (own_ref, 1), (hs_ref, 2), (hs_ref, 3)]
    for p, conv in enumerate(conv_pairs(planes, (1, 3), kf_ref, cells, deep)):
        q = gate(conv)
        sconv_ref[p] = slope(conv, q)
        if p in (1, 2):
            mixed_ref[:, (p - 1) * cells : p * cells] = (conv * q).astype(BF).T


def backward_kernel(
    mode,
    m,
    sent_slot,
    tail_start,
    wide,
    deep,
    taps,
    width,
    x_ref,
    ct_ref,
    cta_ref,
    cta2_ref,
    w_ref,
    rw_ref,
    kb_ref,
    spre_ref,
    sconv_ref,
    *rest,
):
    c = lax.axis_index("chan")
    cells = wide * deep
    tail = pl.ds(tail_start, cells)
    full = mode == "full"
    if mode == "first":
        base_ref, other_ref, gs_ref, br_ref = rest
        up_ref = ct_ref.at[m]
        halo, halo2 = cta_ref[tail], cta2_ref[tail]
        own = (ct_ref[m, 0], ct_ref[m, 1])
    else:
        st_ref, st2_ref, dg_ref, dg2_ref, *rest = rest
        if full:
            hid_ref, mixed_ref, exp_in, red_in, kg_in, *rest = rest
            part_ref, up_ref, exp_ref, red_ref, kg_ref, gs_ref = rest
        else:
            base_ref, other_ref, gs_ref, br_ref, up_ref = rest
        here = pl.ds(sent_slot * cells, cells)
        last = lax.axis_index("section") == lax.axis_size("section") - 1

        mine, theirs = st_ref[here], st2_ref[here]
        own = (
            jnp.where(last, ct_ref[m, 0], jnp.where(c == 0, mine, theirs)),
            jnp.where(last, ct_ref[m, 1], jnp.where(c == 0, theirs, mine)),
        )
        for p in (0, 1):
            up_ref[p] = own[p]
        halo = jnp.where(last, cta_ref[tail], dg_ref[here])
        halo2 = jnp.where(last, cta2_ref[tail], dg2_ref[here])
    below = jnp.where(c == 0, halo2, halo)
    above = jnp.where(c == 0, halo, halo2)
    for plane, up in enumerate((below, *own, above)):
        grad = nt_dot(up, rw_ref[...]) * sconv_ref[plane]
        store_shifts(gs_ref, plane, grad.astype(BF).astype(F32), wide, deep)
    if full:
        ups2 = up_ref[...].reshape(2 * cells, LANES)
        red = jnp.dot(mixed_ref[...], ups2, preferred_element_type=F32)
        red_ref[...] = red_in[...] + red
        groups = LANES // width
        keep = diagonal_mask(width)
        left = hid_ref[...]
        right = []
        for p in (0, 1):
            parts = [
                gs_ref[p + dx, dy * deep : dy * deep + cells, :]
                for dx in range(3)
                for dy in range(3)
            ]
            right.append(jnp.concatenate(parts, axis=1))
        dense = jnp.dot(left, jnp.concatenate(right, axis=0), preferred_element_type=F32)
        for tap in range(taps):
            block = dense[:, tap * LANES : (tap + 1) * LANES].reshape(groups, width, LANES)
            thin = jnp.sum(jnp.where(keep, block, 0.0), axis=0)
            at = slice((taps - 1 - tap) * width, (taps - tap) * width)
            kg_ref[at] = kg_in[at] + thin
    planes = [(gs_ref, p) for p in range(4)]
    grads = []
    for p, grad_hidden in enumerate(conv_pairs(planes, (1,), kb_ref, cells, deep)):
        grad_pre = (grad_hidden * spre_ref[p]).astype(BF)
        branch = nt_dot(grad_pre, w_ref[...])
        if full:
            part_ref[p] = branch.astype(BF)
            grads.append(grad_pre)
        else:
            br_ref[p] = branch
    if full:
        exp_ref[...] = exp_in[...] + jnp.dot(
            x_ref[m], jnp.concatenate(grads, axis=0), preferred_element_type=F32
        )
    else:
        base_ref[...] = up_ref[c].astype(F32) + br_ref[c]
        other_ref[...] = br_ref[1 - c].astype(BF)


def emit_kernel(micro, *refs):
    ins, out_ref = refs[:-1], refs[-1]
    for m in range(micro):
        up, mine, other = ins[3 * m : 3 * m + 3]
        both = mine[...].astype(F32) + other[...].astype(F32)
        out_ref[m] = (up[...].astype(F32) + both).astype(BF)


def finish_kernel(count, scale, taps, width, *refs):
    ins, outs, thin_ref = refs[:count], refs[count:-1], refs[-1]
    total = ins[0][...].astype(F32)
    for ref in ins[1:]:
        total = total + ref[...].astype(F32)
    total = total * scale
    outs[0][...] = total[0:LANES]
    outs[1][...] = total[LANES : 2 * LANES]
    thin_ref[0 : taps * width] = total[2 * LANES :]
    for i in range(width):
        turned = thin_ref[pl.ds(i, LANES, stride=width), :].T
        outs[2][:, i] = turned[:, :taps].reshape(LANES // width, width, taps)


def SENDS(micro):
    return [[0], list(range(1, micro))] if micro > 1 else [[0]]


def sds(shape, dtype):
    return jax.ShapeDtypeStruct(shape, dtype)


def params(mebibytes):
    return pltpu.CompilerParams(vmem_limit_bytes=mebibytes * 2**20)


def call(kernel, name, out_shape, args, scratch=(), in_specs=None, room=16):
    vmem = pl.BlockSpec(memory_space=pltpu.VMEM)
    outs = [vmem] * len(out_shape)
    return pl.pallas_call(
        kernel,
        in_specs=[vmem] * len(args) if in_specs is None else in_specs,
        out_specs=outs,
        out_shape=out_shape,
        scratch_shapes=list(scratch),
        name=name,
        cost_estimate=pl.CostEstimate(flops=2 * 10**9, bytes_accessed=4 * 2**20, transcendentals=0),
        compiler_params=params(room),
    )(*args)


def on_device(
    section_inputs, cotangent, phase_labels, expand_weight, phase_code, kernel, reduce_weight
):
    _, micro, depth, wide, deep, trunk = section_inputs.shape
    cells = wide * deep
    taps, groups, width = kernel.shape[1], kernel.shape[2], kernel.shape[3]
    assert depth == 2 and lax.axis_size("chan") == 2
    assert trunk == LANES and groups * width == LANES
    spaces, sections = lax.axis_size("space"), lax.axis_size("section")
    scale = 1.0 / math.sqrt(micro * depth * spaces * cells)

    x = section_inputs[0].reshape(micro, depth, cells, trunk)
    ct = cotangent.reshape(micro, depth, cells, trunk)
    w, rw = expand_weight[0], reduce_weight[0]
    code = jnp.pad(phase_code[0], ((0, 8 - phase_code.shape[1]), (0, 0)))
    kern = kernel[0].transpose(1, 2, 3, 0)

    away = [(k, c, (k + 2 * c - 1) % spaces) for k in range(spaces) for c in (0, 1)]
    back = [(k, c, (k - 2 * c + 1) % spaces) for k in range(spaces) for c in (0, 1)]
    route_a = [(2 * k + c, 2 * t + c) for k, c, t in away]
    route_b = [(2 * k + c, 2 * t + c) for k, c, t in back]
    route_d = [
        ((k * sections + s) * 2 + c, (t * sections + (s - 1) % sections) * 2 + c)
        for k, c, t in away
        for s in range(sections)
    ]
    route_s = [(s, (s - 1) % sections) for s in range(sections)]

    def swap(v):
        return lax.ppermute(v, "chan", [(0, 1), (1, 0)])

    rows = cells + wide
    hbm = pl.BlockSpec(memory_space=pltpu.HBM)
    packed_a, packed_b, lab = call(
        functools.partial(pack_kernel, micro, cells, wide),
        "pack",
        [
            sds((micro * rows + cells, LANES), BF),
            sds((micro * rows, LANES), BF),
            sds((micro, depth, deep, LANES), BF),
        ],
        (x, ct, phase_labels),
        [
            pltpu.VMEM(phase_labels.shape, jnp.int32),
            pltpu.SemaphoreType.DMA((2 * micro + 2,)),
        ],
        [hbm, hbm, hbm],
        60,
    )
    plane2, plane4, flat = (2, cells, LANES), (4, cells, LANES), (cells, LANES)
    pad_rows = cells + 2 * deep
    square, thin = (LANES, LANES), (taps * width, LANES)
    dense_f, dense_b = call(
        functools.partial(weights_kernel, taps, width),
        "weights",
        [sds((4 * taps // 3 * LANES, 2 * LANES), BF)] * 2,
        (kern,),
        [pltpu.VMEM((LANES * width, LANES), F32), pltpu.VMEM((2,) + thin, F32)],
    )
    *owned, x, ct, w, rw, code, edge, flip = call(
        functools.partial(own_kernel, micro, wide, deep),
        "own",
        [sds((2, pad_rows, 3 * LANES), BF), sds((LANES, 2 * cells), BF), sds(plane2, F32)]
        * micro
        + [sds(v.shape, v.dtype) for v in (x, ct, w, rw, code)]
        + [sds((max(1, micro - 1) * cells, LANES), BF), sds((micro, LANES, 2 * cells), BF)],
        (x, ct, lab, w, rw, code),
    )
    a = lax.ppermute(packed_a, ("space", "chan"), route_a)
    b = lax.ppermute(packed_b, ("space", "chan"), route_b)
    a, b, dense_f, dense_b, *owned = lax.optimization_barrier((a, b, dense_f, dense_b, *owned))
    halos = (a, b, swap(a), swap(b))
    edge = lax.ppermute(edge, ("space", "chan"), route_a)

    def joined(pairs):
        outs = [(base + swap(other).astype(F32)).astype(BF) for base, other in pairs]
        return outs[0] if len(outs) == 1 else jnp.concatenate(outs, axis=0)

    def send_on(out):
        st = lax.ppermute(out, "section", route_s)
        dg = lax.ppermute(out, ("space", "section", "chan"), route_d)
        return st, dg

    def after(arrays, first):
        *arrays, _ = lax.optimization_barrier((*arrays, first))
        return arrays

    def shared(st, dg):
        return st, swap(st), dg, swap(dg)

    def back_pass(mode, m, extra, extra_out=()):
        outs = [sds(flat, F32), sds(flat, BF)] if mode != "full" else [sds(plane2, BF)] * 2
        scratch = [pltpu.VMEM((4, pad_rows, 3 * LANES), BF)]
        if mode != "full":
            scratch.append(pltpu.VMEM(plane2, F32))
        if mode == "light":
            scratch.append(pltpu.VMEM(plane2, BF))
        return call(
            functools.partial(backward_kernel, mode, m, sent_slot[m], tails[m], wide, deep, taps, width),
            "backward_" + mode,
            outs + list(extra_out),
            (flip, ct, *edges[m], w, rw, dense_b, spre[m], sconv[m], *extra),
            scratch,
        )

    sconv, mixed, sent = [], [], []
    sends = SENDS(micro)
    sender = [n for n, group in enumerate(sends) for _ in group]
    sent_slot = [i for group in sends for i in range(len(group))]
    spre = [owned[3 * m + 2] for m in range(micro)]
    tails = [micro * rows] + [m * cells for m in range(micro - 1)]
    edges = [(halos[0], halos[2])]
    pending, previous = [], None
    for m in range(micro):
        con, mix = call(
            functools.partial(forward_kernel, m, wide, deep),
            "forward",
            [sds(plane4, F32), sds((LANES, 2 * cells), BF)],
            (owned[3 * m], *halos, w, code, dense_f),
            [pltpu.VMEM((4, pad_rows, 3 * LANES), BF)],
        )
        sconv.append(con)
        mixed.append(mix)
        (code,) = after((code,), con)
        if m == 0:
            previous = back_pass("first", 0, ())
            (code,) = after((code,), previous[1])
            sent.append(send_on(joined([previous])))
    (edge,) = after((edge,), sconv[-1])
    edges += [(edge, swap(edge))] * (micro - 1)
    waiting = []
    for m in range(1, micro):
        (sconv[m],) = after((sconv[m],), previous[1])
        previous = back_pass("first", m, ())
        waiting.append(previous)
    sent.append(send_on(joined(waiting)))
    sent[0] = after(sent[0], previous[1])
    ups = [shared(*pair) for pair in sent]

    rank = lax.axis_index("section")
    for stage in range(1, sections - 1):
        fresh = []
        for group in sends:
            out = joined([back_pass("light", m, ups[sender[m]]) for m in group])
            fresh.append(shared(*send_on(out)))
        mine = rank == sections - 2 - stage
        ups = [
            tuple(jnp.where(mine, n, o) for n, o in zip(new, old)) for new, old in zip(fresh, ups)
        ]
    sum_shapes = [sds(s, F32) for s in (square, square, thin)]
    sums = [jnp.zeros(s.shape, F32) for s in sum_shapes]
    pieces = []
    for m in range(micro):
        extra = (*ups[sender[m]], owned[3 * m + 1], mixed[m], *sums)
        part, up, *sums = back_pass("full", m, extra, sum_shapes)
        if m == 0 and sections == 2 and sender[-1] > 0:
            ups[-1] = shared(*after(sent[-1], part))
        pieces += [up, part, swap(part)]

    grads = jnp.concatenate([s.astype(BF) for s in sums], axis=0)
    if spaces == 4:
        near = [(k, k ^ 1) for k in range(spaces)]
        far = [(k, k ^ 3) for k in range(spaces)]
        grads = grads + lax.ppermute(grads, "space", near)
        copies = [grads, lax.ppermute(grads, "space", far)]
    else:
        copies = [lax.psum(grads, "space")]
    (out,) = call(
        functools.partial(emit_kernel, micro), "emit", [sds((micro,) + plane2, BF)], pieces
    )
    *copies, out = lax.optimization_barrier((*copies, out))
    exp_g, red_g, kg = call(
        functools.partial(finish_kernel, len(copies), scale, taps, width),
        "finish",
        [sds(square, F32), sds(square, F32), sds((groups, width, width, taps), F32)],
        copies,
        [pltpu.VMEM((LANES * width, LANES), F32)],
    )
    kg = kg.transpose(3, 0, 1, 2)
    return (
        out.reshape(section_inputs.shape),
        exp_g[None],
        kg[None],
        red_g[None],
    )


def solution(mesh):
    placed = (
        P("section", "parts", "space", None, None, None),
        P("parts", "space", None, None, None),
        P("parts", "space", None, None),
        P("section", None, "chan"),
        P("section", None, "chan"),
        P("section", None, "chan", None, None),
        P("section", "chan", None),
    )
    return jax.shard_map(
        on_device,
        mesh=mesh,
        in_specs=placed,
        out_specs=(
            P("section", "parts", "space", None, None, None),
            P(("parts", "section"), None, "chan"),
            P(("parts", "section"), None, "chan", None, None),
            P(("parts", "section"), "chan", None),
        ),
        check_vma=False,
    )
```
